32 devices in a mesh: tm: 2 (over y), height: 16 (over z, x, core).
Axes of the slice: x: 2, y: 2, z: 4, core: 2. Of those that a mesh axis runs over, the one named last changes fastest.
Arguments:
- activations: bfloat16 [4, 64, 256, 128], P('tm', 'height'), may hold values from -60 to 60
- norm_gain: float32 [128], replicated, may hold values from 0.1 to 1.9
- norm_bias: float32 [128], replicated, may hold values from -3 to 3
- conv_weight: bfloat16 [3456, 256], replicated, may hold values from -0.109375 to 0.109375
- cotangent: bfloat16 [2, 64, 256, 256], P('tm', 'height'), may hold values from -6 to 6
Outputs:
- pooled: bfloat16 [2, 64, 256, 256], P('tm', None, 'height')
- weight_grad: bfloat16 [256, 3456], P('height')
The draws below stay inside these ranges and needn't reach their ends.
All inputs are finite; a program needn't handle non-finite values.
Results may differ from the reference program's by a relative error of at most 0.0056.
Values may be sent and summed in bfloat16 or wider, within the bound.
A program may use at most 128 MiB of HBM per device.

```python
import math
import jax
import jax.numpy as jnp
from jax import lax

CIN = 128
COUT = 256
GROUPS = 32
KT = 3
W_COLS = 256
FRAMES = 4
ROWS = 64
FO = 2


def draw_activations(key, part):
    key_noise, key_rough, key_offset, key_factor, key_drift = jax.random.split(key, 5)
    frame_pos = jnp.arange(FRAMES, dtype=jnp.float32) / FRAMES
    row_pos = jnp.arange(ROWS, dtype=jnp.float32) / ROWS
    col_pos = jnp.arange(W_COLS, dtype=jnp.float32) / W_COLS
    level = (frame_pos[:, None, None] + row_pos[None, :, None] + col_pos[None, None, :]) / 3.0
    rough = jax.random.uniform(key_rough, (FRAMES, ROWS, W_COLS), jnp.float32, -0.35, 0.35)
    scale = jnp.exp(2.302585 * level + rough)
    group_factor = jax.random.uniform(key_factor, (GROUPS,), jnp.float32, 0.5, 1.0)
    chan_factor = jnp.repeat(group_factor, CIN // GROUPS)
    amplitude = jax.random.uniform(key_drift, (CIN,), jnp.float32, 0.5, 2.0)
    drift = (frame_pos[:, None, None, None] + row_pos[None, :, None, None]) * 0.5 * amplitude
    noise = jnp.clip(jax.random.normal(key_noise, (FRAMES, ROWS, W_COLS, CIN), jnp.float32), -3.5, 3.5)
    offset = jax.random.uniform(key_offset, (CIN,), jnp.float32, -1.0, 1.0)
    values = noise * scale[:, :, :, None] * chan_factor + offset + drift
    return values.astype(jnp.bfloat16)


def shard_levels(own_key, shape, cuts, least, top_value):
    factor_of = 1.0
    for position, blocks in cuts:
        steps = jax.random.uniform(jax.random.fold_in(jax.random.fold_in(own_key, 6), position), (blocks,), jnp.float32, least / len(cuts), top_value / len(cuts))
        factor_of = factor_of * jnp.repeat(jnp.exp(steps), shape[position] // blocks).reshape((-1,) + (1,) * (len(shape) - 1 - position))
    return factor_of


def centred(key, dims, deviation, bound, cuts=(), kind=jnp.bfloat16):
    array = deviation * jax.random.normal(key, dims, jnp.float32)
    if cuts:
        array = array * shard_levels(key, dims, cuts, -0.22, 0.18)
    return jnp.clip(array, -bound, bound).astype(kind)


def setup_inputs(seed: int = 0) -> dict:
    key_list = jax.random.split(jax.random.key(seed), 6)
    return {
        "activations": draw_activations(jax.random.fold_in(key_list[5], 71), 0),
        "norm_gain": jnp.clip(1.0 + 0.18 * jax.random.normal(key_list[1], (CIN,), jnp.float32), 0.1, 1.9),
        "norm_bias": centred(key_list[2], (CIN,), 0.5, 3.0, (), jnp.float32),
        "conv_weight": centred(key_list[3], (KT * KT * KT * CIN, COUT), (KT * KT * KT * CIN) ** -0.5, 0.109375),
        "cotangent": centred(key_list[4], (FO, ROWS, W_COLS, COUT), 1.0, 6.0, ((0, 2), (1, 16))),
    }


def reference(activations, norm_gain, norm_bias, conv_weight, cotangent):
    per_group = CIN // GROUPS
    grouped = activations.astype(jnp.float32).reshape(-1, GROUPS, per_group)
    group_mean = lax.optimization_barrier(jnp.mean(grouped, axis=(0, 2)))
    centered = grouped - group_mean[None, :, None]
    group_var = lax.optimization_barrier(jnp.mean(centered * centered, axis=(0, 2)))
    mean_chan = jnp.repeat(group_mean, per_group)
    inv_chan = jnp.repeat(lax.rsqrt(group_var + 1e-06), per_group)
    normed = jax.nn.silu((activations.astype(jnp.float32) - mean_chan) * inv_chan * norm_gain + norm_bias).astype(jnp.bfloat16)
    stacked = jnp.concatenate([normed[:1], normed[:1], normed], axis=0)
    padded = jnp.pad(stacked, ((0, 0), (1, 1), (1, 1), (0, 0)))
    upsampled = jnp.repeat(cotangent * jnp.asarray(0.5, jnp.bfloat16), 2, axis=0)

    def frame_step(total, index):
        window = lax.dynamic_slice_in_dim(padded, index, KT, 0)
        pieces = []
        for tap_t in range(KT):
            for tap_r in range(KT):
                for tap_c in range(KT):
                    pieces.append(window[tap_t, tap_r:tap_r + ROWS, tap_c:tap_c + W_COLS])
        patches = jnp.concatenate(pieces, axis=2).reshape(ROWS * W_COLS, KT * KT * KT * CIN)
        frame_out = jnp.dot(patches, conv_weight, preferred_element_type=jnp.float32).astype(jnp.bfloat16)
        upstream = lax.dynamic_index_in_dim(upsampled, index, 0, keepdims=False).reshape(ROWS * W_COLS, COUT)
        total = total + jnp.dot(patches.T, upstream, preferred_element_type=jnp.float32)
        return (total, frame_out.reshape(ROWS, W_COLS, COUT))
    total, conv_out = lax.scan(frame_step, jnp.zeros((KT * KT * KT * CIN, COUT), jnp.float32), jnp.arange(FRAMES, dtype=jnp.int32))
    pairs = conv_out.reshape(FO, 2, ROWS, W_COLS, COUT).astype(jnp.float32)
    pooled = ((pairs[:, 0] + pairs[:, 1]) * 0.5).astype(jnp.bfloat16).transpose(0, 1, 3, 2)
    weight_grad = (total.T * (1.0 / math.sqrt(FRAMES * ROWS * W_COLS))).astype(jnp.bfloat16)
    return (pooled, weight_grad)
```

```python
import functools
import math

import jax
import jax.numpy as jnp
from jax import lax
from jax.experimental import pallas as pl
from jax.experimental.pallas import tpu as pltpu
from jax.sharding import PartitionSpec as P

GROUPS = 32
KT = 3
MESH = pl.DeviceIdType.MESH
ANY = pl.BlockSpec(memory_space=pl.ANY)
VMEM = pl.BlockSpec(memory_space=pltpu.VMEM)
BF16 = jnp.bfloat16
F32 = jnp.float32


def group_total(row, per_group):
    lane = lax.broadcasted_iota(jnp.int32, row.shape, 1)
    count = row.shape[1]
    span = 1
    while span < per_group:
        low = (lane % (2 * span)) < span
        row = row + jnp.where(low, pltpu.roll(row, count - span, 1), pltpu.roll(row, span, 1))
        span *= 2
    return row


def index_of(inner, a, b, core):
    return (a * inner + b) * 2 + core


class Stream:
    def __init__(self, dims, place, refs, sems):
        self.dims, self.place = dims, place
        self.grad, self.got1, self.sum1, self.got2, self.sum2, self.got3, self.part, self.final = refs
        self.send_sem, self.recv_sem = sems

    def remote(self, src, dst, index, to):
        return pltpu.make_async_remote_copy(
            src_ref=src,
            dst_ref=dst,
            send_sem=self.send_sem.at[index],
            recv_sem=self.recv_sem.at[index],
            device_id=to,
            device_id_type=MESH,
        )

    def start_pair(self):
        n_time, n_rows, outer, inner = self.dims
        time, height, a, b, core = self.place
        self.pair = self.remote(self.grad.at[1 - core], self.got1, 0, (time, index_of(inner, a, b, 1 - core)))
        self.pair.start()

    def start_second(self):
        n_time, n_rows, outer, inner = self.dims
        time, height, a, b, core = self.place
        self.pair.wait()
        for t in range(n_time):
            for b_ in range(inner):
                for a_ in range(outer):
                    self.sum1[t, b_, a_] = (
                        self.grad[core, t, b_, a_].astype(F32) + self.got1[t, b_, a_].astype(F32)
                    ).astype(BF16)
        self.seconds = []
        for dt in range(n_time):
            for db in range(inner):
                if dt or db:
                    slot = dt * inner + db - 1
                    t_, b_ = (time + dt) % n_time, (b + db) % inner
                    self.seconds.append(
                        self.remote(
                            self.sum1.at[t_, b_], self.got2.at[slot], 1 + slot, (t_, index_of(inner, a, b_, core))
                        )
                    )
        for copy in self.seconds:
            copy.start()

    def start_third(self):
        n_time, n_rows, outer, inner = self.dims
        time, height, a, b, core = self.place
        for copy in self.seconds:
            copy.wait_recv()
        for a_ in range(outer):
            total = self.grad[core, time, b, a_].astype(F32) + self.got1[time, b, a_].astype(F32)
            for slot in range(n_time * inner - 1):
                total = total + self.got2[slot, a_].astype(F32)
            self.sum2[a_] = total.astype(BF16)
        self.thirds = []
        for step in range(1, outer):
            a_ = (a + step) % outer
            self.thirds.append(
                self.remote(
                    self.sum2.at[a_],
                    self.got3.at[step - 1],
                    n_time * inner + step - 1,
                    (time, index_of(inner, a_, b, core)),
                )
            )
        for copy in self.thirds:
            copy.start()

    def start_last(self, factor):
        n_time, n_rows, outer, inner = self.dims
        time, height, a, b, core = self.place
        for copy in self.thirds:
            copy.wait_recv()
        total = self.sum2[a].astype(F32)
        for step in range(1, outer):
            total = total + self.got3[step - 1].astype(F32)
        self.part[...] = (total * factor).astype(BF16)
        self.final[time] = self.part[...]
        self.base = n_time * inner + outer - 1
        self.lasts = []
        for t in range(1, n_time):
            self.lasts.append(
                self.remote(self.part, self.final.at[time], self.base + t - 1, ((time + t) % n_time, height))
            )
        for copy in self.lasts:
            copy.start()

    def finish(self):
        n_time = self.dims[0]
        time, height = self.place[:2]
        for t in range(1, n_time):
            sender = (time + n_time - t) % n_time
            self.remote(self.part, self.final.at[sender], self.base + t - 1, (sender, height)).wait_recv()
        whole = jnp.concatenate([self.final[t] for t in range(n_time)], axis=1)
        for copy in self.seconds + self.thirds + self.lasts:
            copy.wait_send()
        return whole


def block_kernel(dims, factor, act, gain_in, bias_in, weight_in, cot_in, out, wgrad, *scratch):
    n_time, n_rows, outer, inner = dims
    full, taps, acc, alone, gain, bias, weight, cot, cot_next, cot_t, next_t, mine, stats, pooled = scratch[:14]
    local_sem, halo_send, halo_recv, stat_send, stat_recv, block_send, block_recv = scratch[14:21]
    late_refs, late_sems = scratch[21:29], scratch[29:31]
    early_refs, early_sems = scratch[31:39], scratch[39:41]
    time, height = lax.axis_index("tm"), lax.axis_index("height")
    frames, rows, width, channels = act.shape
    n_out = weight.shape[1]
    own_rows = n_out // n_rows
    pixels = rows * width
    band = KT * KT * channels
    n_dev = n_time * n_rows
    me = time * n_rows + height
    core, q = height % 2, height // 2
    place = (time, height, q // inner, q % inner, core)
    late = Stream(dims, place, late_refs, late_sems)
    early = Stream(dims, place, early_refs, early_sems)
    has_up, has_down = height > 0, height < n_rows - 1
    has_next, has_prev = time < n_time - 1, time > 0

    own_frames, old_frames = pl.ds(frames, frames), pl.ds(0, frames)
    loads = [
        pltpu.make_async_copy(act, full.at[own_frames, pl.ds(1, rows)], local_sem.at[0]),
        pltpu.make_async_copy(gain_in, gain, local_sem.at[1]),
        pltpu.make_async_copy(bias_in, bias, local_sem.at[2]),
        pltpu.make_async_copy(cot_in, cot, local_sem.at[3]),
        pltpu.make_async_copy(weight_in, weight, local_sem.at[4]),
    ]
    for load in loads:
        load.start()

    barrier = pltpu.get_barrier_semaphore()

    def greet(step, carry):
        other = (me + step) % n_dev
        pl.semaphore_signal(barrier, inc=1, device_id=(other // n_rows, other % n_rows), device_id_type=MESH)
        return carry

    lax.fori_loop(1, n_dev, greet, 0)

    loads[0].wait()
    local = frames * pixels
    chan_sum = jnp.zeros((1, channels), F32)
    for f in range(frames):
        for r in range(rows):
            chan_sum = chan_sum + jnp.sum(full[frames + f, 1 + r].astype(F32), axis=0, keepdims=True)
    chan_mean = chan_sum * (1.0 / local)
    chan_dev = jnp.zeros((1, channels), F32)
    for f in range(frames):
        for r in range(rows):
            away = full[frames + f, 1 + r].astype(F32) - chan_mean
            chan_dev = chan_dev + jnp.sum(away * away, axis=0, keepdims=True)
    packed = jnp.concatenate([chan_mean, chan_dev], axis=0)
    mine[...] = packed
    stats[me] = packed
    loads[3].wait()
    with jax.named_scope("entry"):
        pl.semaphore_wait(barrier, n_dev - 1)

    def stat(step, slot, to_time, to_height):
        return pltpu.make_async_remote_copy(
            src_ref=mine,
            dst_ref=stats.at[slot],
            send_sem=stat_send.at[step],
            recv_sem=stat_recv.at[step],
            device_id=(to_time, to_height),
            device_id_type=MESH,
        )

    def stat_out(step):
        return stat(step, me, (time + step // n_rows) % n_time, (height + step % n_rows) % n_rows)

    def send(step, carry):
        stat_out(step).start()
        return carry

    def old_rows(row, count):
        return full.at[own_frames, pl.ds(row, count)], full.at[old_frames, pl.ds(row, count)]

    moves = [
        (*old_rows(rows, 1), 1, 0, has_next, has_prev),
        (*old_rows(1, 1), 1, 0, has_next, has_prev),
        (*old_rows(2, 1), 1, 0, has_next, has_prev),
        (*old_rows(3, rows - 3), 1, 0, has_next, has_prev),
        (full.at[own_frames, pl.ds(1, 1)], full.at[own_frames, pl.ds(rows + 1, 1)], 0, -1, has_up, has_down),
        (full.at[own_frames, pl.ds(rows, 1)], full.at[own_frames, pl.ds(0, 1)], 0, 1, has_down, has_up),
        (
            full.at[old_frames, pl.ds(rows, 1)],
            full.at[old_frames, pl.ds(0, 1)],
            0,
            1,
            has_prev & has_down,
            has_prev & has_up,
        ),
        (
            full.at[old_frames, pl.ds(1, 1)],
            full.at[old_frames, pl.ds(rows + 1, 1)],
            0,
            -1,
            has_prev & has_up,
            has_prev & has_down,
        ),
        (cot.at[pl.ds(1, rows - 1)], cot_next, -1, 0, has_prev, has_next),
    ]

    def halo(index):
        source, target, frame_step, row_step = moves[index][:4]
        return pltpu.make_async_remote_copy(
            src_ref=source,
            dst_ref=target,
            send_sem=halo_send.at[index],
            recv_sem=halo_recv.at[index],
            device_id=(time + frame_step, height + row_step),
            device_id_type=MESH,
        )

    def start(index):
        pl.when(moves[index][4])(lambda: halo(index).start())

    def arrived(index):
        pl.when(moves[index][5])(lambda: halo(index).wait_recv())

    with jax.named_scope("sends"):
        lax.fori_loop(1, n_dev, send, 0)
        for index in (4, 5, 0, 1, 2, 3, 8):
            start(index)

    zero_rows = jnp.zeros((2 * frames, 1, width, channels), BF16)

    @pl.when(jnp.logical_not(has_up))
    def _():
        full[:, pl.ds(0, 1)] = zero_rows

    @pl.when(jnp.logical_not(has_down))
    def _():
        full[:, pl.ds(rows + 1, 1)] = zero_rows

    for y in range(rows):
        cot_t[:, y * width : (y + 1) * width] = cot[y].astype(F32).T.astype(BF16)
    for index in (1, 2, 4):
        loads[index].wait()

    def receive(step, carry):
        from_time = (time + n_time - step // n_rows) % n_time
        from_height = (height + n_rows - step % n_rows) % n_rows
        stat(step, from_time * n_rows + from_height, from_time, from_height).wait_recv()
        return carry

    with jax.named_scope("stats_in"):
        lax.fori_loop(1, n_dev, receive, 0)
    per_group = channels // GROUPS
    means, devs = stats[:, 0], stats[:, 1]
    mean = group_total(jnp.sum(means, axis=0, keepdims=True), per_group) * (1.0 / (n_dev * per_group))
    away = means - mean
    spread = jnp.sum(devs + local * (away * away), axis=0, keepdims=True)
    var = group_total(spread, per_group) * (1.0 / (local * n_dev * per_group))
    scale = lax.rsqrt(var + 1e-06) * gain[...]
    shift = bias[...]
    column = lax.broadcasted_iota(jnp.int32, (width, channels), 0)

    def normed(f, r):
        inside = jnp.logical_and(r + height > 0, r + height * rows < n_rows * rows + 1)
        v = (full[f, r].astype(F32) - mean) * scale + shift
        v = v / (1.0 + jnp.exp(-v))
        return v.astype(BF16).astype(F32) * inside.astype(F32)

    def line(r):
        return pl.ds(pl.multiple_of(r * width, width), width)

    def put(t, r, value):
        left = jnp.where(column == 0, 0.0, pltpu.roll(value, 1, 0))
        right = jnp.where(column == width - 1, 0.0, pltpu.roll(value, width - 1, 0))
        taps[t, line(r), 0:channels] = left.astype(BF16)
        taps[t, line(r), channels : 2 * channels] = value.astype(BF16)
        taps[t, line(r), 2 * channels :] = right.astype(BF16)

    OLD, MIXED, OWN, ONE, TWO = range(5)

    def prepare_own(r, carry):
        one, two = normed(frames, r), normed(frames + 1, r)
        put(OWN, r, one + two)
        put(ONE, r, one)
        put(TWO, r, two)
        return carry

    def prepare_old(r, carry):
        one, two = normed(0, r), normed(1, r)
        put(OLD, r, one + two)
        put(MIXED, r, two + taps[ONE, line(r), channels : 2 * channels].astype(F32))
        return carry

    def repeat_first(r, carry):
        twice = (taps[ONE, line(r), :].astype(F32) * 2.0).astype(BF16)
        taps[OLD, line(r), :] = twice
        taps[MIXED, line(r), :] = twice
        return carry

    with jax.named_scope("halo_own"):
        arrived(4)
        arrived(5)
    with jax.named_scope("prep_own"):
        lax.fori_loop(0, rows + 2, prepare_own, 0)

    def windows(t, y, count):
        return [taps[t, (y + r) * width : (y + r + count) * width] for r in range(KT)]

    def gradient(lhs, t, y, count):
        return jnp.dot(lhs, jnp.concatenate(windows(t, y, count), axis=1), preferred_element_type=F32)

    def store(stream, total, offset, length):
        total = total.astype(BF16)
        span = stream.grad.shape[-1]
        for piece in range(n_time):
            begin, end = max(offset, piece * span), min(offset + band, (piece + 1) * span)
            if begin < end:
                part = total[:, begin - offset : end - offset]
                for block in range(n_rows):
                    q_, core_ = block // 2, block % 2
                    stream.grad[
                        core_, piece, q_ % inner, q_ // inner, :, begin - piece * span : end - piece * span
                    ] = part[block * own_rows : (block + 1) * own_rows]
            unused = max(length, piece * span) - piece * span
            if offset + band == length and unused < span:
                stream.grad[:, piece, :, :, :, unused:] = jnp.zeros((2, inner, outer, own_rows, span - unused), BF16)

    with jax.named_scope("halo_relay"):
        arrived(0)
        start(6)
    with jax.named_scope("grad_own"):
        store(early, gradient(cot_t[...], OWN, 0, rows), 0, band)
        early.start_pair()
    with jax.named_scope("halo_relay2"):
        arrived(1)
        start(7)

    many = 2 if rows % 2 == 0 else 1

    def conv_own(y, carry):
        patch = [taps[OWN, pl.ds(pl.multiple_of((y * many + r) * width, width), many * width)] for r in range(KT)]
        acc[pl.ds(pl.multiple_of(y * many * width, width), many * width), :] = jnp.dot(
            jnp.concatenate(patch, axis=1), weight[2 * band :], preferred_element_type=F32
        )
        return carry

    with jax.named_scope("grad_alone"):
        alone[...] = gradient(cot_t[:, width:], ONE, 1, rows - 1)
    with jax.named_scope("conv_own"):
        lax.fori_loop(0, rows // many, conv_own, 0)
    with jax.named_scope("early2"):
        early.start_second()

    with jax.named_scope("halo_old_a"):
        arrived(2)
        arrived(6)
    with jax.named_scope("prep_old_a"):

        @pl.when(has_prev)
        def _():
            lax.fori_loop(0, 3, prepare_old, 0)

        @pl.when(jnp.logical_not(has_prev))
        def _():
            lax.fori_loop(0, rows + 2, repeat_first, 0)

    def conv_old(y, count):
        lhs = jnp.concatenate(windows(OLD, y, count) + windows(MIXED, y, count), axis=1)
        total = jnp.dot(lhs, weight[0 : 2 * band], preferred_element_type=F32)
        total = (acc[y * width : (y + count) * width, :] + total) * 0.5
        for k in range(count):
            part = total[k * width : (k + 1) * width].T.astype(BF16)
            pooled[:, y + k] = part.reshape(n_rows, own_rows, width)

    groups = [(0, 1), (1, rows - 1)]

    def block(group, step, slot, other):
        y, count = groups[group]
        index = group * n_rows + step
        return pltpu.make_async_remote_copy(
            src_ref=pooled.at[other, pl.ds(y, count)],
            dst_ref=out.at[pl.ds(slot * rows + y, count)],
            send_sem=block_send.at[index],
            recv_sem=block_recv.at[index],
            device_id=(time, other),
            device_id_type=MESH,
        )

    def spread_out(group):
        for step in range(1, n_rows):
            block(group, step, height, (height + step) % n_rows).start()

    with jax.named_scope("conv_a"):
        conv_old(0, 1)
        spread_out(0)

    with jax.named_scope("cot_next"):
        arrived(8)

    once = jnp.where(has_prev, 1.0, 2.0).astype(F32)
    extra = jnp.where(has_prev, 0.0, 2.0).astype(F32)

    def late_term(t, factor_alone, next_t_of, offset):
        total = alone[...] * factor_alone + gradient(cot_t[:, :width], t, 0, 1)

        @pl.when(has_next)
        def _():
            store(late, total + gradient(next_t[...], next_t_of, 1, rows - 1), offset, 2 * band)

        @pl.when(jnp.logical_not(has_next))
        def _():
            store(late, total, offset, 2 * band)

    with jax.named_scope("grad_late"):

        @pl.when(has_next)
        def _():
            for y in range(rows - 1):
                next_t[:, y * width : (y + 1) * width] = cot_next[y].astype(F32).T.astype(BF16)

        late_term(OLD, extra, OWN, 0)
        late_term(MIXED, once, TWO, band)
        late.start_pair()

    with jax.named_scope("halo_old_b"):
        arrived(3)
        arrived(7)
    with jax.named_scope("prep_old_b"):

        @pl.when(has_prev)
        def _():
            lax.fori_loop(3, rows + 2, prepare_old, 0)
    with jax.named_scope("late2"):
        late.start_second()
    with jax.named_scope("conv_b"):
        conv_old(1, rows - 1)
        spread_out(1)

    out[pl.ds(height * rows, rows)] = pooled[height]
    with jax.named_scope("early3"):
        early.start_third()
    with jax.named_scope("late3"):
        late.start_third()
    with jax.named_scope("early4"):
        early.start_last(factor)
        wgrad[:, 2 * band :] = early.finish()[:, :band]
    with jax.named_scope("late4"):
        late.start_last(factor)
    with jax.named_scope("late5"):
        wgrad[:, : 2 * band] = late.finish()[:, : 2 * band]

    with jax.named_scope("blocks_in"):
        for group in range(len(groups)):
            for step in range(1, n_rows):
                sender = (height + n_rows - step) % n_rows
                block(group, step, sender, sender).wait_recv()
                block(group, step, height, (height + step) % n_rows).wait_send()
    for index in range(len(moves)):
        pl.when(moves[index][4])(functools.partial(lambda i: halo(i).wait_send(), index))

    def sent(step, carry):
        stat_out(step).wait_send()
        return carry

    lax.fori_loop(1, n_dev, sent, 0)


def deliver_kernel(block_in, grad_in, block_out, grad_out, sem):
    copies = [
        pltpu.make_async_copy(block_in, block_out, sem.at[0]),
        pltpu.make_async_copy(grad_in, grad_out, sem.at[1]),
    ]
    for copy in copies:
        copy.start()
    for copy in copies:
        copy.wait()


def local(activations, norm_gain, norm_bias, conv_weight, cotangent):
    frames, rows, width, channels = activations.shape
    depth, n_out = conv_weight.shape
    n_time, n_rows = lax.axis_size("tm"), lax.axis_size("height")
    n_dev = n_time * n_rows
    inner = 2
    outer = n_rows // (2 * inner)
    own_rows = n_out // n_rows
    dims = (n_time, n_rows, outer, inner)
    dma = pltpu.SemaphoreType.DMA
    factor = 0.5 / math.sqrt(frames * n_time * rows * n_rows * width)

    def stream(length):
        span = -(-length // (128 * n_time)) * 128
        n_sems = n_time * inner + outer + n_time
        shapes = [
            (2, n_time, inner, outer, own_rows, span),
            (n_time, inner, outer, own_rows, span),
            (n_time, inner, outer, own_rows, span),
            (n_time * inner - 1, outer, own_rows, span),
            (outer, own_rows, span),
            (outer - 1, own_rows, span),
            (own_rows, span),
            (n_time, own_rows, span),
        ]
        return [pltpu.VMEM(shape, BF16) for shape in shapes] + [dma((n_sems,)), dma((n_sems,))]

    band = depth // KT
    out, weight_grad = pl.pallas_call(
        functools.partial(block_kernel, dims, factor),
        out_shape=(
            pltpu.VMEM((rows * n_rows, own_rows, width), BF16),
            pltpu.VMEM((own_rows, depth), BF16),
        ),
        in_specs=[ANY] * 5,
        out_specs=(VMEM, VMEM),
        scratch_shapes=[
            pltpu.VMEM((2 * frames, rows + 2, width, channels), BF16),
            pltpu.VMEM((5, (rows + 2) * width, KT * channels), BF16),
            pltpu.VMEM((rows * width, n_out), F32),
            pltpu.VMEM((n_out, band), F32),
            pltpu.VMEM((1, channels), F32),
            pltpu.VMEM((1, channels), F32),
            pltpu.VMEM((depth, n_out), BF16),
            pltpu.VMEM((rows, width, n_out), BF16),
            pltpu.VMEM((rows - 1, width, n_out), BF16),
            pltpu.VMEM((n_out, rows * width), BF16),
            pltpu.VMEM((n_out, (rows - 1) * width), BF16),
            pltpu.VMEM((2, channels), F32),
            pltpu.VMEM((n_dev, 2, channels), F32),
            pltpu.VMEM((n_rows, rows, own_rows, width), BF16),
            dma((5,)),
            dma((9,)),
            dma((9,)),
            dma((n_dev,)),
            dma((n_dev,)),
            dma((2 * n_rows,)),
            dma((2 * n_rows,)),
            *stream(2 * band),
            *stream(band),
        ],
        compiler_params=pltpu.CompilerParams(collective_id=0, has_side_effects=True, vmem_limit_bytes=60 << 20),
        name="block",
    )(
        activations,
        norm_gain.reshape(1, channels),
        norm_bias.reshape(1, channels),
        conv_weight,
        cotangent.reshape(rows, width, n_out),
    )
    out, weight_grad = pl.pallas_call(
        deliver_kernel,
        out_shape=(
            jax.ShapeDtypeStruct(out.shape, BF16),
            jax.ShapeDtypeStruct(weight_grad.shape, BF16),
        ),
        in_specs=[ANY] * 2,
        out_specs=(ANY, ANY),
        scratch_shapes=[dma((2,))],
        compiler_params=pltpu.CompilerParams(vmem_limit_bytes=4 << 20),
        name="deliver",
    )(out, weight_grad)
    return (out.reshape((1,) + out.shape), weight_grad)


def solution(mesh):
    in_specs = (P("tm", "height", None, None), P(), P(), P(), P("tm", "height", None, None))
    out_specs = (P("tm", None, "height", None), P("height", None))
    return jax.shard_map(local, mesh=mesh, in_specs=in_specs, out_specs=out_specs, check_vma=False)
```

```python
import functools
import math

import jax
import jax.numpy as jnp
from jax import lax
from jax.experimental import pallas as pl
from jax.experimental.pallas import tpu as pltpu
from jax.sharding import PartitionSpec as P

GROUPS = 32
MARGIN = 16
KT = 3
MESH = pl.DeviceIdType.MESH
ANY = pl.BlockSpec(memory_space=pl.ANY)
VMEM = pl.BlockSpec(memory_space=pltpu.VMEM)
BF16 = jnp.bfloat16
F32 = jnp.float32


def group_total(row, per_group):
    lane = lax.broadcasted_iota(jnp.int32, row.shape, 1)
    count = row.shape[1]
    span = 1
    while span < per_group:
        low = (lane % (2 * span)) < span
        row = row + jnp.where(low, pltpu.roll(row, count - span, 1), pltpu.roll(row, span, 1))
        span *= 2
    return row


def index_of(inner, a, b, core):
    return (a * inner + b) * 2 + core


class Stream:
    def __init__(self, dims, place, rows_first, refs, sems):
        self.dims, self.place, self.rows_first = dims, place, rows_first
        self.grad, self.got1, self.sum1, self.got2, self.sum2, self.got3, self.sum3, self.got4, self.part, self.final = refs
        self.send_sem, self.recv_sem = sems
        self.used, self.started = 0, []

    def remote(self, src, dst, index, to):
        return pltpu.make_async_remote_copy(
            src_ref=src,
            dst_ref=dst,
            send_sem=self.send_sem.at[index],
            recv_sem=self.recv_sem.at[index],
            device_id=to,
            device_id_type=MESH,
        )

    def begin(self, copies):
        self.current = [self.remote(src, dst, self.used + i, to) for i, (src, dst, to) in enumerate(copies)]
        self.used += len(copies)
        for copy in self.current:
            copy.start()
        self.started += self.current

    def wait(self):
        for copy in self.current:
            copy.wait_recv()

    def over_rows(self, source, target):
        n_time, n_rows, outer, inner = self.dims
        time, height, a, b, core = self.place
        copies = []
        for step in range(1, inner):
            b_ = (b + step) % inner
            copies.append((source(b_), target.at[step - 1], (time, index_of(inner, a, b_, core))))
        self.begin(copies)

    def over_time(self, source, target):
        n_time, n_rows, outer, inner = self.dims
        time, height, a, b, core = self.place
        copies = []
        for step in range(1, n_time):
            t_ = (time + step) % n_time
            copies.append((source(t_), target.at[step - 1], (t_, height)))
        self.begin(copies)

    def start_pair(self):
        n_time, n_rows, outer, inner = self.dims
        time, height, a, b, core = self.place
        self.begin([(self.grad.at[1 - core], self.got1, (time, index_of(inner, a, b, 1 - core)))])

    def start_second(self):
        n_time, n_rows, outer, inner = self.dims
        core = self.place[4]
        self.wait()
        for t in range(n_time):
            for b_ in range(inner):
                for a_ in range(outer):
                    self.sum1[t, b_, a_] = (
                        self.grad[core, t, b_, a_].astype(F32) + self.got1[t, b_, a_].astype(F32)
                    ).astype(BF16)
        if self.rows_first:
            self.over_rows(lambda b_: self.sum1.at[:, b_], self.got2)
        else:
            self.over_time(lambda t_: self.sum1.at[t_], self.got2)

    def start_third(self):
        n_time, n_rows, outer, inner = self.dims
        time, height, a, b, core = self.place
        self.wait()
        mine = (lambda i, a_: self.sum1[i, b, a_]) if self.rows_first else (lambda i, a_: self.sum1[time, i, a_])
        for i in range(n_time if self.rows_first else inner):
            for a_ in range(outer):
                total = mine(i, a_).astype(F32)
                for slot in range(self.got2.shape[0]):
                    total = total + self.got2[slot, i, a_].astype(F32)
                self.sum2[i, a_] = total.astype(BF16)
        if self.rows_first:
            self.over_time(lambda t_: self.sum2.at[t_], self.got3)
        else:
            self.over_rows(lambda b_: self.sum2.at[b_], self.got3)

    def start_fourth(self):
        n_time, n_rows, outer, inner = self.dims
        time, height, a, b, core = self.place
        self.wait()
        mine = time if self.rows_first else b
        for a_ in range(outer):
            total = self.sum2[mine, a_].astype(F32)
            for slot in range(self.got3.shape[0]):
                total = total + self.got3[slot, a_].astype(F32)
            self.sum3[a_] = total.astype(BF16)
        copies = []
        for step in range(1, outer):
            a_ = (a + step) % outer
            copies.append((self.sum3.at[a_], self.got4.at[step - 1], (time, index_of(inner, a_, b, core))))
        self.begin(copies)

    def start_last(self, factor):
        n_time, n_rows, outer, inner = self.dims
        time, height, a, b, core = self.place
        self.wait()
        total = self.sum3[a].astype(F32)
        for step in range(1, outer):
            total = total + self.got4[step - 1].astype(F32)
        self.part[...] = (total * factor).astype(BF16)
        self.final[time] = self.part[...]
        self.base = self.used
        self.begin(
            [(self.part, self.final.at[time], ((time + step) % n_time, height)) for step in range(1, n_time)]
        )

    def finish(self):
        n_time = self.dims[0]
        time, height = self.place[:2]
        for t in range(1, n_time):
            sender = (time + n_time - t) % n_time
            self.remote(self.part, self.final.at[sender], self.base + t - 1, (sender, height)).wait_recv()
        whole = jnp.concatenate([self.final[t] for t in range(n_time)], axis=1)
        for copy in self.started:
            copy.wait_send()
        return whole


def block_kernel(dims, cut, factor, act, gain_in, bias_in, weight_in, cot_in, out, wgrad, *scratch):
    n_time, n_rows, outer, inner = dims
    full, taps, alone, gain, bias, weight, cot, cot_next, cot_t, next_t, mine, stats, pooled = scratch[:13]
    local_sem, halo_send, halo_recv, stat_sem, block_sem = scratch[13:18]
    time, height = lax.axis_index("tm"), lax.axis_index("height")
    frames, rows, width, channels = act.shape
    n_out = weight.shape[1]
    own_rows = n_out // n_rows
    pixels = rows * width
    half, edge = width // 2, width // 2 + MARGIN
    area = rows * half
    band = KT * KT * channels
    n_dev = n_time * n_rows
    me = time * n_rows + height
    core, q = height % 2, height // 2
    place = (time, height, q // inner, q % inner, core)
    late_a, late_b, early = (
        Stream(dims, place, rows_first, scratch[i : i + 10], scratch[i + 10 : i + 12])
        for i, rows_first in ((18, True), (30, False), (42, True))
    )
    parts = [(late_b, 0, cut), (late_a, cut, 2 * band), (early, 2 * band, 3 * band)]
    has_up, has_down = height > 0, height < n_rows - 1
    has_next, has_prev = time < n_time - 1, time > 0

    own_frames, old_frames = pl.ds(frames, frames), pl.ds(0, frames)
    loads = [
        pltpu.make_async_copy(act, full.at[own_frames, pl.ds(1, rows)], local_sem.at[0]),
        pltpu.make_async_copy(gain_in, gain, local_sem.at[1]),
        pltpu.make_async_copy(bias_in, bias, local_sem.at[2]),
        pltpu.make_async_copy(cot_in, cot, local_sem.at[3]),
        pltpu.make_async_copy(weight_in, weight, local_sem.at[4]),
    ]
    for load in loads:
        load.start()

    barrier = pltpu.get_barrier_semaphore()
    def peer(step):
        other = (me + step) % n_dev
        return other // n_rows, other % n_rows

    def greet(step, carry):
        pl.semaphore_signal(barrier, inc=1, device_id=peer(step), device_id_type=MESH)
        return carry

    lax.fori_loop(1, n_dev, greet, 0)

    loads[0].wait()
    local = frames * pixels
    chan_sum = jnp.zeros((1, channels), F32)
    for f in range(frames):
        for r in range(rows):
            chan_sum = chan_sum + jnp.sum(full[frames + f, 1 + r].astype(F32), axis=0, keepdims=True)
    chan_mean = chan_sum * (1.0 / local)
    chan_dev = jnp.zeros((1, channels), F32)
    for f in range(frames):
        for r in range(rows):
            away = full[frames + f, 1 + r].astype(F32) - chan_mean
            chan_dev = chan_dev + jnp.sum(away * away, axis=0, keepdims=True)
    packed = jnp.concatenate([chan_mean, chan_dev], axis=0)
    mine[...] = packed
    stats[me] = packed
    loads[3].wait()
    with jax.named_scope("entry"):
        pl.semaphore_wait(barrier, n_dev - 1)

    def send(step, carry):
        pltpu.make_async_remote_copy(
            src_ref=mine,
            dst_ref=stats.at[me],
            send_sem=stat_sem.at[0],
            recv_sem=stat_sem.at[1],
            device_id=peer(step),
            device_id_type=MESH,
        ).start()
        return carry

    def taken(ref, sem):
        pltpu.make_async_copy(ref, ref, sem).wait()

    def own_to_old(row, count, begin, end):
        place_in = (pl.ds(row, count), pl.ds(begin, end - begin))
        return full.at[own_frames, *place_in], full.at[old_frames, *place_in]

    def relay(row, to_row, begin, end):
        columns = pl.ds(begin, end - begin)
        return full.at[old_frames, pl.ds(row, 1), columns], full.at[old_frames, pl.ds(to_row, 1), columns]

    moves = [
        (*own_to_old(rows, 1, 0, edge), 1, 0, has_next, has_prev),
        (*own_to_old(1, 1, 0, edge), 1, 0, has_next, has_prev),
        (*own_to_old(2, rows - 2, 0, edge), 1, 0, has_next, has_prev),
        (*own_to_old(rows, 1, edge, width), 1, 0, has_next, has_prev),
        (*own_to_old(1, 1, edge, width), 1, 0, has_next, has_prev),
        (*own_to_old(2, rows - 2, edge, width), 1, 0, has_next, has_prev),
        (full.at[own_frames, pl.ds(1, 1)], full.at[own_frames, pl.ds(rows + 1, 1)], 0, -1, has_up, has_down),
        (full.at[own_frames, pl.ds(rows, 1)], full.at[own_frames, pl.ds(0, 1)], 0, 1, has_down, has_up),
        (*relay(rows, 0, 0, edge), 0, 1, has_prev & has_down, has_prev & has_up),
        (*relay(1, rows + 1, 0, edge), 0, -1, has_prev & has_up, has_prev & has_down),
        (*relay(rows, 0, edge, width), 0, 1, has_prev & has_down, has_prev & has_up),
        (*relay(1, rows + 1, edge, width), 0, -1, has_prev & has_up, has_prev & has_down),
        (cot.at[:, pl.ds(half, half)], cot_next, -1, 0, has_prev, has_next),
    ]

    def halo(index):
        source, target, frame_step, row_step = moves[index][:4]
        return pltpu.make_async_remote_copy(
            src_ref=source,
            dst_ref=target,
            send_sem=halo_send.at[index],
            recv_sem=halo_recv.at[index],
            device_id=(time + frame_step, height + row_step),
            device_id_type=MESH,
        )

    def start(index):
        pl.when(moves[index][4])(lambda: halo(index).start())

    def arrived(index):
        pl.when(moves[index][5])(lambda: halo(index).wait_recv())

    with jax.named_scope("sends"):
        lax.fori_loop(1, n_dev, send, 0)
        for index in (6, 7, 0, 1, 12, 2, 3, 4, 5):
            start(index)

    zero_rows = jnp.zeros((2 * frames, 1, width, channels), BF16)

    @pl.when(jnp.logical_not(has_up))
    def _():
        full[:, pl.ds(0, 1)] = zero_rows

    @pl.when(jnp.logical_not(has_down))
    def _():
        full[:, pl.ds(rows + 1, 1)] = zero_rows

    for y in range(rows):
        turned = cot[y].astype(F32).T.astype(BF16)
        for side in range(2):
            cot_t[:, side * area + y * half : side * area + (y + 1) * half] = turned[:, side * half : (side + 1) * half]
    for index in (1, 2, 4):
        loads[index].wait()

    with jax.named_scope("halo_relay"):
        arrived(0)
        start(8)
    with jax.named_scope("stats_in"):
        taken(stats.at[pl.ds(0, n_dev - 1)], stat_sem.at[1])
    per_group = channels // GROUPS
    means, devs = stats[:, 0], stats[:, 1]
    mean = group_total(jnp.sum(means, axis=0, keepdims=True), per_group) * (1.0 / (n_dev * per_group))
    away = means - mean
    spread = jnp.sum(devs + local * (away * away), axis=0, keepdims=True)
    var = group_total(spread, per_group) * (1.0 / (local * n_dev * per_group))
    scale = lax.rsqrt(var + 1e-06) * gain[...]
    shift = bias[...]
    column = lax.broadcasted_iota(jnp.int32, (edge, channels), 0)

    def normed(f, r, side):
        inside = jnp.logical_and(r + height > 0, r + height * rows < n_rows * rows + 1)
        v = (full[f, r, side * (width - edge) : side * (width - edge) + edge].astype(F32) - mean) * scale + shift
        v = v / (1.0 + jnp.exp(-v))
        return v.astype(BF16).astype(F32) * inside.astype(F32)

    def line(r):
        return pl.ds(pl.multiple_of(r * half, half), half)

    def put(t, side, r, value):
        left, right = pltpu.roll(value, 1, 0), pltpu.roll(value, edge - 1, 0)
        if side == 0:
            left = jnp.where(column == 0, 0.0, left)
        else:
            right = jnp.where(column == edge - 1, 0.0, right)
        for c, part in enumerate((left, value, right)):
            taps[t, side, line(r), c * channels : (c + 1) * channels] = part[
                side * MARGIN : side * MARGIN + half
            ].astype(BF16)

    OLD, MIXED, OWN, ONE, TWO = range(5)

    def prepare_own(r, carry):
        for side in range(2):
            one, two = normed(frames, r, side), normed(frames + 1, r, side)
            put(OWN, side, r, one + two)
            put(ONE, side, r, one)
            put(TWO, side, r, two)
        return carry

    def prepare_old(side):
        def body(r, carry):
            one, two = normed(0, r, side), normed(1, r, side)
            put(OLD, side, r, one + two)
            put(MIXED, side, r, two + normed(frames, r, side))
            return carry

        @pl.when(has_prev)
        def _():
            lax.fori_loop(0, rows + 2, body, 0)

    def repeat_first(r, carry):
        for side in range(2):
            twice = (taps[ONE, side, line(r), :].astype(F32) * 2.0).astype(BF16)
            taps[OLD, side, line(r), :] = twice
            taps[MIXED, side, line(r), :] = twice
        return carry

    with jax.named_scope("halo_own"):
        arrived(6)
        arrived(7)
    with jax.named_scope("prep_own"):
        lax.fori_loop(0, rows + 2, prepare_own, 0)

    def windows(t, side):
        return [taps[t, side, r * half : r * half + area] for r in range(KT)]

    def gradient(lhs, t, side):
        return jnp.dot(lhs, jnp.concatenate(windows(t, side), axis=1), preferred_element_type=F32)

    left_t, right_t = cot_t.at[:, pl.ds(0, area)], cot_t.at[:, pl.ds(area, area)]

    def store(t, total):
        total = total.astype(BF16)
        for stream, first, last in parts:
            span = stream.grad.shape[-1]
            for piece in range(n_time):
                lead = first + piece * span
                begin, end = max(lead, t * band), min(lead + span, last, (t + 1) * band)
                if begin < end:
                    part = total[:, begin - t * band : end - t * band]
                    for block in range(n_rows):
                        q_, core_ = block // 2, block % 2
                        stream.grad[core_, piece, q_ % inner, q_ // inner, :, begin - lead : end - lead] = part[
                            block * own_rows : (block + 1) * own_rows
                        ]
                unused = max(last, lead) - lead
                if unused < span and (last - 1) // band == t:
                    stream.grad[:, piece, :, :, :, unused:] = jnp.zeros(
                        (2, inner, outer, own_rows, span - unused), BF16
                    )

    def conv(side):
        lhs = jnp.concatenate([piece for t in (OLD, MIXED, OWN) for piece in windows(t, side)], axis=1)
        total = jnp.dot(lhs, weight[...], preferred_element_type=F32) * 0.5
        for y in range(rows):
            part = total[y * half : (y + 1) * half].T.astype(BF16)
            pooled[:, y, :, side * half : (side + 1) * half] = part.reshape(n_rows, own_rows, half)

    def spread_out(side, crossing):
        columns = pl.ds(side * half, half)
        for cross in range(1, inner) if crossing else [0]:
            for lag in range(outer):
                for core_ in range(2):
                    if cross or lag or core_:
                        other = index_of(
                            inner, (place[2] + lag) % outer, (place[3] + cross) % inner, (core + core_) % 2
                        )
                        pltpu.make_async_remote_copy(
                            src_ref=pooled.at[other, :, :, columns],
                            dst_ref=out.at[pl.ds(height * rows, rows), :, columns],
                            send_sem=block_sem.at[0],
                            recv_sem=block_sem.at[1],
                            device_id=(time, other),
                            device_id_type=MESH,
                        ).start()

    @pl.when(jnp.logical_not(has_prev))
    def _():
        with jax.named_scope("repeat_first"):
            lax.fori_loop(0, rows + 2, repeat_first, 0)

    with jax.named_scope("halo_relay2"):
        arrived(1)
        start(9)
    with jax.named_scope("grad_own"):
        store(2, gradient(left_t[...], OWN, 0) + gradient(right_t[...], OWN, 1))
        early.start_pair()
    with jax.named_scope("grad_alone"):
        alone[...] = gradient(right_t[...], ONE, 1)

    @pl.when(jnp.logical_not(has_prev))
    def _():
        with jax.named_scope("conv_first_a"):
            conv(0)

    with jax.named_scope("early2"):
        early.start_second()

    @pl.when(jnp.logical_not(has_prev))
    def _():
        spread_out(0, False)

    with jax.named_scope("cot_next"):
        arrived(12)

        @pl.when(has_next)
        def _():
            for y in range(rows):
                next_t[:, y * half : (y + 1) * half] = cot_next[y].astype(F32).T.astype(BF16)

    with jax.named_scope("halo_old_a"):
        for index in (2, 8, 9):
            arrived(index)
    with jax.named_scope("prep_old_a"):
        prepare_old(0)

    once = jnp.where(has_prev, 1.0, 2.0).astype(F32)
    extra = jnp.where(has_prev, 0.0, 2.0).astype(F32)

    def late_term(t, factor_alone, next_t_of):
        total = alone[...] * factor_alone + gradient(left_t[...], t, 0)

        @pl.when(has_next)
        def _():
            store(t, total + gradient(next_t[...], next_t_of, 1))

        @pl.when(jnp.logical_not(has_next))
        def _():
            store(t, total)

    with jax.named_scope("grad_late"):
        late_term(MIXED, once, TWO)
        late_term(OLD, extra, OWN)
        late_b.start_pair()
        late_a.start_pair()
    with jax.named_scope("halo_relay3"):
        arrived(3)
        start(10)

    with jax.named_scope("conv_1st"):

        @pl.when(has_prev)
        def _():
            conv(0)
            arrived(4)
            start(11)
            spread_out(0, False)

        @pl.when(jnp.logical_not(has_prev))
        def _():
            conv(1)
            spread_out(1, False)

    with jax.named_scope("late2"):
        late_b.start_second()
        late_a.start_second()
    spread_out(0, True)
    with jax.named_scope("halo_old_b"):
        for index in (5, 10, 11):
            arrived(index)
    with jax.named_scope("prep_old_b"):
        prepare_old(1)

    @pl.when(has_prev)
    def _():
        with jax.named_scope("conv_b"):
            conv(1)
            spread_out(1, False)

    with jax.named_scope("early3"):
        early.start_third()
    out[pl.ds(height * rows, rows)] = pooled[height]
    with jax.named_scope("late3a"):
        late_a.start_third()
    with jax.named_scope("late3b"):
        late_b.start_third()

    @pl.when(jnp.logical_not(has_prev))
    def _():
        spread_out(1, True)

    with jax.named_scope("early4"):
        early.start_fourth()
    with jax.named_scope("late4a"):
        late_a.start_fourth()
    with jax.named_scope("late4b"):
        late_b.start_fourth()

    @pl.when(has_prev)
    def _():
        spread_out(1, True)

    with jax.named_scope("last"):
        for stream in (early, late_a, late_b):
            stream.start_last(factor)
    with jax.named_scope("finish"):
        for stream, first, last in parts:
            wgrad[:, first:last] = stream.finish()[:, : last - first]

    with jax.named_scope("blocks_in"):
        taken(out.at[pl.ds(0, (n_rows - 1) * rows)], block_sem.at[1])
    with jax.named_scope("sent"):
        taken(out.at[pl.ds(0, (n_rows - 1) * rows)], block_sem.at[0])
        taken(stats.at[pl.ds(0, n_dev - 1)], stat_sem.at[0])
        for index in range(len(moves)):
            pl.when(moves[index][4])(functools.partial(lambda i: halo(i).wait_send(), index))


def deliver_kernel(block_in, grad_in, block_out, grad_out, sem):
    copies = [
        pltpu.make_async_copy(block_in, block_out, sem.at[0]),
        pltpu.make_async_copy(grad_in, grad_out, sem.at[1]),
    ]
    for copy in copies:
        copy.start()
    for copy in copies:
        copy.wait()


def local(activations, norm_gain, norm_bias, conv_weight, cotangent):
    frames, rows, width, channels = activations.shape
    depth, n_out = conv_weight.shape
    n_time, n_rows = lax.axis_size("tm"), lax.axis_size("height")
    n_dev = n_time * n_rows
    inner = 2
    outer = n_rows // (2 * inner)
    own_rows = n_out // n_rows
    dims = (n_time, n_rows, outer, inner)
    dma = pltpu.SemaphoreType.DMA
    factor = 0.5 / math.sqrt(frames * n_time * rows * n_rows * width)

    def stream(length, rows_first):
        span = -(-length // (128 * n_time)) * 128
        n_sems = 1 + inner + outer + 2 * n_time
        steps = [n_time, inner] if rows_first else [inner, n_time]
        chunk = (outer, own_rows, span)
        shapes = [
            (2, n_time, inner, *chunk),
            (n_time, inner, *chunk),
            (n_time, inner, *chunk),
            (steps[1] - 1, steps[0], *chunk),
            (steps[0], *chunk),
            (steps[0] - 1, *chunk),
            chunk,
            (outer - 1, own_rows, span),
            (own_rows, span),
            (n_time, own_rows, span),
        ]
        return [pltpu.VMEM(shape, BF16) for shape in shapes] + [dma((n_sems,)), dma((n_sems,))]

    band = depth // KT
    cut = 8 * channels
    out, weight_grad = pl.pallas_call(
        functools.partial(block_kernel, dims, cut, factor),
        out_shape=(
            pltpu.VMEM((rows * n_rows, own_rows, width), BF16),
            pltpu.VMEM((own_rows, depth), BF16),
        ),
        in_specs=[ANY] * 5,
        out_specs=(VMEM, VMEM),
        scratch_shapes=[
            pltpu.VMEM((2 * frames, rows + 2, width, channels), BF16),
            pltpu.VMEM((5, 2, (rows + 2) * (width // 2), KT * channels), BF16),
            pltpu.VMEM((n_out, band), F32),
            pltpu.VMEM((1, channels), F32),
            pltpu.VMEM((1, channels), F32),
            pltpu.VMEM((depth, n_out), BF16),
            pltpu.VMEM((rows, width, n_out), BF16),
            pltpu.VMEM((rows, width // 2, n_out), BF16),
            pltpu.VMEM((n_out, rows * width), BF16),
            pltpu.VMEM((n_out, rows * (width // 2)), BF16),
            pltpu.VMEM((2, channels), F32),
            pltpu.VMEM((n_dev, 2, channels), F32),
            pltpu.VMEM((n_rows, rows, own_rows, width), BF16),
            dma((5,)),
            dma((13,)),
            dma((13,)),
            dma((2,)),
            dma((2,)),
            *stream(2 * band - cut, True),
            *stream(cut, False),
            *stream(band, True),
        ],
        compiler_params=pltpu.CompilerParams(collective_id=0, has_side_effects=True, vmem_limit_bytes=60 << 20),
        name="block",
    )(
        activations,
        norm_gain.reshape(1, channels),
        norm_bias.reshape(1, channels),
        conv_weight,
        cotangent.reshape(rows, width, n_out),
    )
    out, weight_grad = pl.pallas_call(
        deliver_kernel,
        out_shape=(
            jax.ShapeDtypeStruct(out.shape, BF16),
            jax.ShapeDtypeStruct(weight_grad.shape, BF16),
        ),
        in_specs=[ANY] * 2,
        out_specs=(ANY, ANY),
        scratch_shapes=[dma((2,))],
        compiler_params=pltpu.CompilerParams(vmem_limit_bytes=4 << 20),
        name="deliver",
    )(out, weight_grad)
    return (out.reshape((1,) + out.shape), weight_grad)


def solution(mesh):
    in_specs = (P("tm", "height", None, None), P(), P(), P(), P("tm", "height", None, None))
    out_specs = (P("tm", None, "height", None), P("height", None))
    return jax.shard_map(local, mesh=mesh, in_specs=in_specs, out_specs=out_specs, check_vma=False)
```

```python
import functools
import math

import jax
import jax.numpy as jnp
from jax import lax
from jax.experimental import pallas as pl
from jax.experimental.pallas import tpu as pltpu
from jax.sharding import PartitionSpec as P

GROUPS = 32
MARGIN = 16
KT = 3
MESH = pl.DeviceIdType.MESH
ANY = pl.BlockSpec(memory_space=pl.ANY)
VMEM = pl.BlockSpec(memory_space=pltpu.VMEM)
BF16 = jnp.bfloat16
F32 = jnp.float32


def group_total(row, per_group):
    lane = lax.broadcasted_iota(jnp.int32, row.shape, 1)
    count = row.shape[1]
    span = 1
    while span < per_group:
        low = (lane % (2 * span)) < span
        row = row + jnp.where(low, pltpu.roll(row, count - span, 1), pltpu.roll(row, span, 1))
        span *= 2
    return row


def index_of(inner, a, b, core):
    return (a * inner + b) * 2 + core


def taken(ref, sem):
    pltpu.make_async_copy(ref, ref, sem).wait()


class Stream:
    def __init__(self, dims, place, rows_first, refs, sems):
        self.dims, self.place, self.rows_first = dims, place, rows_first
        self.grad, self.got1, self.sum1, self.got2, self.sum2, self.got3, self.sum3, self.got4, self.part, self.final = refs
        self.send_sem, self.recv_sem = sems
        self.step = 0

    def begin(self, copies):
        for src, dst, to in copies:
            pltpu.make_async_remote_copy(
                src_ref=src,
                dst_ref=dst,
                send_sem=self.send_sem.at[self.step],
                recv_sem=self.recv_sem.at[self.step],
                device_id=to,
                device_id_type=MESH,
            ).start()
        self.step += 1

    def over_rows(self, source, target):
        n_time, n_rows, outer, inner = self.dims
        time, height, a, b, core = self.place
        copies = []
        for step in range(1, inner):
            b_ = (b + step) % inner
            copies.append((source(b_), target.at[step - 1], (time, index_of(inner, a, b_, core))))
        self.begin(copies)

    def over_time(self, source, target):
        n_time, n_rows, outer, inner = self.dims
        time, height, a, b, core = self.place
        copies = []
        for step in range(1, n_time):
            t_ = (time + step) % n_time
            copies.append((source(t_), target.at[step - 1], (t_, height)))
        self.begin(copies)

    def start_pair(self):
        n_time, n_rows, outer, inner = self.dims
        time, height, a, b, core = self.place
        self.begin([(self.grad.at[1 - core], self.got1, (time, index_of(inner, a, b, 1 - core)))])

    def paired(self, t, b_, a_):
        return self.grad[self.place[4], t, b_, a_].astype(F32) + self.got1[t, b_, a_].astype(F32)

    def start_second(self):
        n_time, n_rows, outer, inner = self.dims
        taken(self.got1, self.recv_sem.at[0])
        for t in range(n_time):
            for b_ in range(inner):
                for a_ in range(outer):
                    self.sum1[t, b_, a_] = self.paired(t, b_, a_).astype(BF16)
        if self.rows_first:
            self.over_rows(lambda b_: self.sum1.at[:, b_], self.got2)
        else:
            self.over_time(lambda t_: self.sum1.at[t_], self.got2)

    def start_third(self):
        n_time, n_rows, outer, inner = self.dims
        time, height, a, b, core = self.place
        taken(self.got2, self.recv_sem.at[1])
        for i in range(n_time if self.rows_first else inner):
            for a_ in range(outer):
                total = self.paired(i, b, a_) if self.rows_first else self.paired(time, i, a_)
                for slot in range(self.got2.shape[0]):
                    total = total + self.got2[slot, i, a_].astype(F32)
                self.sum2[i, a_] = total.astype(BF16)
        if self.rows_first:
            self.over_time(lambda t_: self.sum2.at[t_], self.got3)
        else:
            self.over_rows(lambda b_: self.sum2.at[b_], self.got3)

    def start_fourth(self):
        n_time, n_rows, outer, inner = self.dims
        time, height, a, b, core = self.place
        taken(self.got3, self.recv_sem.at[2])
        mine = time if self.rows_first else b
        for a_ in range(outer):
            total = self.sum2[mine, a_].astype(F32)
            for slot in range(self.got3.shape[0]):
                total = total + self.got3[slot, a_].astype(F32)
            self.sum3[a_] = total.astype(BF16)
        copies = []
        for step in range(1, outer):
            a_ = (a + step) % outer
            copies.append((self.sum3.at[a_], self.got4.at[step - 1], (time, index_of(inner, a_, b, core))))
        self.begin(copies)

    def start_last(self, factor):
        n_time, n_rows, outer, inner = self.dims
        time, height, a, b, core = self.place
        taken(self.got4, self.recv_sem.at[3])
        total = self.sum3[a].astype(F32)
        for step in range(1, outer):
            total = total + self.got4[step - 1].astype(F32)
        self.part[...] = (total * factor).astype(BF16)
        self.final[time] = self.part[...]
        self.begin([(self.part, self.final.at[time], ((time + step) % n_time, height)) for step in range(1, n_time)])

    def finish(self):
        n_time = self.dims[0]
        others = self.final.at[pl.ds(0, n_time - 1)]
        taken(others, self.recv_sem.at[4])
        whole = jnp.concatenate([self.final[t] for t in range(n_time)], axis=1)
        for step, ref in enumerate((self.got1, self.got2, self.got3, self.got4, others)):
            taken(ref, self.send_sem.at[step])
        return whole


def block_kernel(dims, cut, factor, act, gain_in, bias_in, weight_in, cot_in, out, wgrad, *scratch):
    n_time, n_rows, outer, inner = dims
    full, taps, alone, gain, bias, weight, cot, cot_next, cot_t, next_t, mine, stats, pooled = scratch[:13]
    local_sem, halo_send, halo_recv, stat_sem, block_sem = scratch[13:18]
    time, height = lax.axis_index("tm"), lax.axis_index("height")
    frames, rows, width, channels = act.shape
    n_out = weight.shape[1]
    own_rows = n_out // n_rows
    pixels = rows * width
    half, edge = width // 2, width // 2 + MARGIN
    area = rows * half
    band = KT * KT * channels
    n_dev = n_time * n_rows
    me = time * n_rows + height
    core, q = height % 2, height // 2
    place = (time, height, q // inner, q % inner, core)
    late_a, late_b, early = (
        Stream(dims, place, rows_first, scratch[i : i + 10], scratch[i + 10 : i + 12])
        for i, rows_first in ((18, True), (30, False), (42, True))
    )
    parts = [(late_b, 0, cut), (late_a, cut, 2 * band), (early, 2 * band, 3 * band)]
    has_up, has_down = height > 0, height < n_rows - 1
    has_next, has_prev = time < n_time - 1, time > 0

    own_frames, old_frames = pl.ds(frames, frames), pl.ds(0, frames)
    loads = [
        pltpu.make_async_copy(act, full.at[own_frames, pl.ds(1, rows)], local_sem.at[0]),
        pltpu.make_async_copy(gain_in, gain, local_sem.at[1]),
        pltpu.make_async_copy(bias_in, bias, local_sem.at[2]),
        pltpu.make_async_copy(cot_in, cot, local_sem.at[3]),
        pltpu.make_async_copy(weight_in, weight, local_sem.at[4]),
    ]
    for load in loads:
        load.start()

    barrier = pltpu.get_barrier_semaphore()
    away_from = 2 * (2 * height // n_rows) - 1

    def peer(step):
        return (time + step // n_rows) % n_time, (height + n_rows + away_from * (step % n_rows)) % n_rows

    def greet(step, carry):
        pl.semaphore_signal(barrier, inc=1, device_id=peer(step), device_id_type=MESH)
        return carry

    for lag in range(1, n_time):
        lax.fori_loop(lag * n_rows + 1, (lag + 1) * n_rows, greet, 0)
        greet(lag * n_rows, 0)
    lax.fori_loop(1, n_rows, greet, 0)

    loads[0].wait()
    local = frames * pixels
    chan_sum = jnp.zeros((1, channels), F32)
    for f in range(frames):
        for r in range(rows):
            chan_sum = chan_sum + jnp.sum(full[frames + f, 1 + r].astype(F32), axis=0, keepdims=True)
    chan_mean = chan_sum * (1.0 / local)
    chan_dev = jnp.zeros((1, channels), F32)
    for f in range(frames):
        for r in range(rows):
            away = full[frames + f, 1 + r].astype(F32) - chan_mean
            chan_dev = chan_dev + jnp.sum(away * away, axis=0, keepdims=True)
    packed = jnp.concatenate([chan_mean, chan_dev], axis=0)
    mine[...] = packed
    stats[me] = packed
    loads[3].wait()
    with jax.named_scope("entry"):
        pl.semaphore_wait(barrier, n_dev - 1)

    def send(step, carry):
        pltpu.make_async_remote_copy(
            src_ref=mine,
            dst_ref=stats.at[me],
            send_sem=stat_sem.at[0],
            recv_sem=stat_sem.at[1],
            device_id=peer(step),
            device_id_type=MESH,
        ).start()
        return carry

    def own_to_old(row, count, begin, end):
        place_in = (pl.ds(row, count), pl.ds(begin, end - begin))
        return full.at[own_frames, *place_in], full.at[old_frames, *place_in]

    def relay(row, to_row, begin, end):
        columns = pl.ds(begin, end - begin)
        return full.at[old_frames, pl.ds(row, 1), columns], full.at[old_frames, pl.ds(to_row, 1), columns]

    moves = [
        (*own_to_old(rows, 1, 0, edge), 1, 0, has_next, has_prev),
        (*own_to_old(1, 1, 0, edge), 1, 0, has_next, has_prev),
        (*own_to_old(2, rows - 2, 0, edge), 1, 0, has_next, has_prev),
        (*own_to_old(rows, 1, edge, width), 1, 0, has_next, has_prev),
        (*own_to_old(1, 1, edge, width), 1, 0, has_next, has_prev),
        (*own_to_old(2, rows - 2, edge, width), 1, 0, has_next, has_prev),
        (full.at[own_frames, pl.ds(1, 1)], full.at[own_frames, pl.ds(rows + 1, 1)], 0, -1, has_up, has_down),
        (full.at[own_frames, pl.ds(rows, 1)], full.at[own_frames, pl.ds(0, 1)], 0, 1, has_down, has_up),
        (*relay(rows, 0, 0, edge), 0, 1, has_prev & has_down, has_prev & has_up),
        (*relay(1, rows + 1, 0, edge), 0, -1, has_prev & has_up, has_prev & has_down),
        (*relay(rows, 0, edge, width), 0, 1, has_prev & has_down, has_prev & has_up),
        (*relay(1, rows + 1, edge, width), 0, -1, has_prev & has_up, has_prev & has_down),
        (cot.at[:, pl.ds(half, half)], cot_next, -1, 0, has_prev, has_next),
    ]

    def halo(index):
        source, target, frame_step, row_step = moves[index][:4]
        return pltpu.make_async_remote_copy(
            src_ref=source,
            dst_ref=target,
            send_sem=halo_send.at[index],
            recv_sem=halo_recv.at[index],
            device_id=(time + frame_step, height + row_step),
            device_id_type=MESH,
        )

    def start(index):
        pl.when(moves[index][4])(lambda: halo(index).start())

    def arrived(index):
        pl.when(moves[index][5])(lambda: halo(index).wait_recv())

    with jax.named_scope("sends"):
        for lag in range(1, n_time):
            lax.fori_loop(lag * n_rows + 1, (lag + 1) * n_rows, send, 0)
            send(lag * n_rows, 0)
        for index in (0, 1, 12, 2, 3, 4, 5):
            start(index)
        lax.fori_loop(1, n_rows, send, 0)
        for index in (6, 7):
            start(index)

    zero_rows = jnp.zeros((2 * frames, 1, width, channels), BF16)

    @pl.when(jnp.logical_not(has_up))
    def _():
        full[:, pl.ds(0, 1)] = zero_rows

    @pl.when(jnp.logical_not(has_down))
    def _():
        full[:, pl.ds(rows + 1, 1)] = zero_rows

    for y in range(rows):
        turned = cot[y].astype(F32).T.astype(BF16)
        for side in range(2):
            cot_t[:, side * area + y * half : side * area + (y + 1) * half] = turned[:, side * half : (side + 1) * half]
    for index in (1, 2, 4):
        loads[index].wait()

    with jax.named_scope("halo_relay"):
        arrived(0)
        start(8)
    with jax.named_scope("stats_in"):
        taken(stats.at[pl.ds(0, n_dev - 1)], stat_sem.at[1])
    per_group = channels // GROUPS
    means, devs = stats[:, 0], stats[:, 1]
    mean = group_total(jnp.sum(means, axis=0, keepdims=True), per_group) * (1.0 / (n_dev * per_group))
    away = means - mean
    spread = jnp.sum(devs + local * (away * away), axis=0, keepdims=True)
    var = group_total(spread, per_group) * (1.0 / (local * n_dev * per_group))
    scale = lax.rsqrt(var + 1e-06) * gain[...]
    shift = bias[...]
    column = lax.broadcasted_iota(jnp.int32, (edge, channels), 0)

    def normed(f, r, side):
        inside = jnp.logical_and(r + height > 0, r + height * rows < n_rows * rows + 1)
        v = (full[f, r, side * (width - edge) : side * (width - edge) + edge].astype(F32) - mean) * scale + shift
        v = v / (1.0 + jnp.exp(-v))
        return v.astype(BF16).astype(F32) * inside.astype(F32)

    def line(r):
        return pl.ds(pl.multiple_of(r * half, half), half)

    def put(t, side, r, value):
        left, right = pltpu.roll(value, 1, 0), pltpu.roll(value, edge - 1, 0)
        if side == 0:
            left = jnp.where(column == 0, 0.0, left)
        else:
            right = jnp.where(column == edge - 1, 0.0, right)
        for c, part in enumerate((left, value, right)):
            taps[t, side, line(r), c * channels : (c + 1) * channels] = part[
                side * MARGIN : side * MARGIN + half
            ].astype(BF16)

    OLD, MIXED, OWN, ONE, TWO = range(5)

    def prepare_own(r, carry):
        for side in range(2):
            one, two = normed(frames, r, side), normed(frames + 1, r, side)
            put(OWN, side, r, one + two)
            put(ONE, side, r, one)
            put(TWO, side, r, two)
        return carry

    def prepare_old(side):
        def body(r, carry):
            one, two = normed(0, r, side), normed(1, r, side)
            put(OLD, side, r, one + two)
            put(MIXED, side, r, two + normed(frames, r, side))
            return carry

        @pl.when(has_prev)
        def _():
            lax.fori_loop(0, rows + 2, body, 0)

    def repeat_first(r, carry):
        for side in range(2):
            twice = (taps[ONE, side, line(r), :].astype(F32) * 2.0).astype(BF16)
            taps[OLD, side, line(r), :] = twice
            taps[MIXED, side, line(r), :] = twice
        return carry

    with jax.named_scope("prep_own"):
        lax.fori_loop(1, rows + 1, prepare_own, 0)
    with jax.named_scope("halo_own"):
        arrived(6)
        arrived(7)
    with jax.named_scope("prep_own_edge"):
        lax.fori_loop(0, 2, lambda i, carry: prepare_own(i * (rows + 1), carry), 0)

    def windows(t, side):
        return [taps[t, side, r * half : r * half + area] for r in range(KT)]

    def gradient(lhs, t, side):
        return jnp.dot(lhs, jnp.concatenate(windows(t, side), axis=1), preferred_element_type=F32)

    left_t, right_t = cot_t.at[:, pl.ds(0, area)], cot_t.at[:, pl.ds(area, area)]

    def store(t, total):
        total = total.astype(BF16)
        for stream, first, last in parts:
            span = stream.grad.shape[-1]
            for piece in range(n_time):
                lead = first + piece * span
                begin, end = max(lead, t * band), min(lead + span, last, (t + 1) * band)
                if begin < end:
                    part = total[:, begin - t * band : end - t * band]
                    for block in range(n_rows):
                        q_, core_ = block // 2, block % 2
                        stream.grad[core_, piece, q_ % inner, q_ // inner, :, begin - lead : end - lead] = part[
                            block * own_rows : (block + 1) * own_rows
                        ]
                unused = max(last, lead) - lead
                if unused < span and (last - 1) // band == t:
                    stream.grad[:, piece, :, :, :, unused:] = jnp.zeros(
                        (2, inner, outer, own_rows, span - unused), BF16
                    )

    def conv(side):
        lhs = jnp.concatenate([piece for t in (OLD, MIXED, OWN) for piece in windows(t, side)], axis=1)
        total = jnp.dot(lhs, weight[...], preferred_element_type=F32) * 0.5
        for y in range(rows):
            part = total[y * half : (y + 1) * half].T.astype(BF16)
            pooled[:, y, :, side * half : (side + 1) * half] = part.reshape(n_rows, own_rows, half)

    def spread_out(side, crossing):
        columns = pl.ds(side * half, half)
        for cross in range(1, inner) if crossing else [0]:
            for lag in range(outer):
                for core_ in range(2):
                    if cross or lag or core_:
                        other = index_of(
                            inner, (place[2] + lag) % outer, (place[3] + cross) % inner, (core + core_) % 2
                        )
                        pltpu.make_async_remote_copy(
                            src_ref=pooled.at[other, :, :, columns],
                            dst_ref=out.at[pl.ds(height * rows, rows), :, columns],
                            send_sem=block_sem.at[0],
                            recv_sem=block_sem.at[1],
                            device_id=(time, other),
                            device_id_type=MESH,
                        ).start()

    @pl.when(jnp.logical_not(has_prev))
    def _():
        with jax.named_scope("repeat_first"):
            lax.fori_loop(0, rows + 2, repeat_first, 0)

    with jax.named_scope("halo_relay2"):
        arrived(1)
        start(9)
    with jax.named_scope("grad_own"):
        store(2, gradient(left_t[...], OWN, 0) + gradient(right_t[...], OWN, 1))
        early.start_pair()
    with jax.named_scope("grad_alone"):
        alone[...] = gradient(right_t[...], ONE, 1)

    @pl.when(jnp.logical_not(has_prev))
    def _():
        with jax.named_scope("conv_first_a"):
            conv(0)

    with jax.named_scope("early2"):
        early.start_second()

    @pl.when(jnp.logical_not(has_prev))
    def _():
        spread_out(0, False)

    with jax.named_scope("cot_next"):
        arrived(12)

        @pl.when(has_next)
        def _():
            for y in range(rows):
                next_t[:, y * half : (y + 1) * half] = cot_next[y].astype(F32).T.astype(BF16)

    with jax.named_scope("halo_old_a"):
        for index in (2, 8, 9):
            arrived(index)
    with jax.named_scope("prep_old_a"):
        prepare_old(0)

    once = jnp.where(has_prev, 1.0, 2.0).astype(F32)
    extra = jnp.where(has_prev, 0.0, 2.0).astype(F32)

    def late_term(t, factor_alone, next_t_of):
        total = alone[...] * factor_alone + gradient(left_t[...], t, 0)

        @pl.when(has_next)
        def _():
            store(t, total + gradient(next_t[...], next_t_of, 1))

        @pl.when(jnp.logical_not(has_next))
        def _():
            store(t, total)

    with jax.named_scope("grad_late"):
        late_term(MIXED, once, TWO)
        late_term(OLD, extra, OWN)
        late_b.start_pair()
        late_a.start_pair()
    with jax.named_scope("halo_relay3"):
        arrived(3)
        start(10)

    with jax.named_scope("conv_1st"):

        @pl.when(has_prev)
        def _():
            conv(0)
            arrived(4)
            start(11)
            spread_out(0, False)

        @pl.when(jnp.logical_not(has_prev))
        def _():
            conv(1)
            spread_out(1, False)

    with jax.named_scope("late2"):
        late_b.start_second()
        late_a.start_second()
    with jax.named_scope("halo_old_b"):
        for index in (5, 10, 11):
            arrived(index)
    with jax.named_scope("prep_old_b"):
        prepare_old(1)

    @pl.when(has_prev)
    def _():
        with jax.named_scope("conv_b"):
            conv(1)
            spread_out(1, False)

    with jax.named_scope("early3"):
        early.start_third()
    out[pl.ds(height * rows, rows)] = pooled[height]
    with jax.named_scope("late3a"):
        late_a.start_third()
    with jax.named_scope("late3b"):
        late_b.start_third()
    with jax.named_scope("early4"):
        early.start_fourth()
    with jax.named_scope("late4a"):
        late_a.start_fourth()
    with jax.named_scope("late4b"):
        late_b.start_fourth()
    spread_out(0, True)
    spread_out(1, True)
    with jax.named_scope("last"):
        early.start_last(factor)
        late_a.start_last(factor)
        late_b.start_last(factor)
    with jax.named_scope("finish"):
        for stream, first, last in parts:
            wgrad[:, first:last] = stream.finish()[:, : last - first]

    with jax.named_scope("blocks_in"):
        taken(out.at[pl.ds(0, (n_rows - 1) * rows)], block_sem.at[1])
    with jax.named_scope("sent"):
        taken(out.at[pl.ds(0, (n_rows - 1) * rows)], block_sem.at[0])
        taken(stats.at[pl.ds(0, n_dev - 1)], stat_sem.at[0])
        for index in range(len(moves)):
            pl.when(moves[index][4])(functools.partial(lambda i: halo(i).wait_send(), index))


def deliver_kernel(block_in, grad_in, block_out, grad_out, sem):
    copies = [
        pltpu.make_async_copy(block_in, block_out, sem.at[0]),
        pltpu.make_async_copy(grad_in, grad_out, sem.at[1]),
    ]
    for copy in copies:
        copy.start()
    for copy in copies:
        copy.wait()


def local(activations, norm_gain, norm_bias, conv_weight, cotangent):
    frames, rows, width, channels = activations.shape
    depth, n_out = conv_weight.shape
    n_time, n_rows = lax.axis_size("tm"), lax.axis_size("height")
    n_dev = n_time * n_rows
    inner = 2
    outer = n_rows // (2 * inner)
    own_rows = n_out // n_rows
    dims = (n_time, n_rows, outer, inner)
    dma = pltpu.SemaphoreType.DMA
    factor = 0.5 / math.sqrt(frames * n_time * rows * n_rows * width)

    def stream(length, rows_first):
        span = -(-length // (128 * n_time)) * 128
        steps = [n_time, inner] if rows_first else [inner, n_time]
        chunk = (outer, own_rows, span)
        shapes = [
            (2, n_time, inner, *chunk),
            (n_time, inner, *chunk),
            (n_time, inner, *chunk),
            (steps[1] - 1, steps[0], *chunk),
            (steps[0], *chunk),
            (steps[0] - 1, *chunk),
            chunk,
            (outer - 1, own_rows, span),
            (own_rows, span),
            (n_time, own_rows, span),
        ]
        return [pltpu.VMEM(shape, BF16) for shape in shapes] + [dma((5,)), dma((5,))]

    band = depth // KT
    cut = 8 * channels
    out, weight_grad = pl.pallas_call(
        functools.partial(block_kernel, dims, cut, factor),
        out_shape=(
            pltpu.VMEM((rows * n_rows, own_rows, width), BF16),
            pltpu.VMEM((own_rows, depth), BF16),
        ),
        in_specs=[ANY] * 5,
        out_specs=(VMEM, VMEM),
        scratch_shapes=[
            pltpu.VMEM((2 * frames, rows + 2, width, channels), BF16),
            pltpu.VMEM((5, 2, (rows + 2) * (width // 2), KT * channels), BF16),
            pltpu.VMEM((n_out, band), F32),
            pltpu.VMEM((1, channels), F32),
            pltpu.VMEM((1, channels), F32),
            pltpu.VMEM((depth, n_out), BF16),
            pltpu.VMEM((rows, width, n_out), BF16),
            pltpu.VMEM((rows, width // 2, n_out), BF16),
            pltpu.VMEM((n_out, rows * width), BF16),
            pltpu.VMEM((n_out, rows * (width // 2)), BF16),
            pltpu.VMEM((2, channels), F32),
            pltpu.VMEM((n_dev, 2, channels), F32),
            pltpu.VMEM((n_rows, rows, own_rows, width), BF16),
            dma((5,)),
            dma((13,)),
            dma((13,)),
            dma((2,)),
            dma((2,)),
            *stream(2 * band - cut, True),
            *stream(cut, False),
            *stream(band, True),
        ],
        compiler_params=pltpu.CompilerParams(collective_id=0, has_side_effects=True, vmem_limit_bytes=60 << 20),
        name="block",
    )(
        activations,
        norm_gain.reshape(1, channels),
        norm_bias.reshape(1, channels),
        conv_weight,
        cotangent.reshape(rows, width, n_out),
    )
    out, weight_grad = pl.pallas_call(
        deliver_kernel,
        out_shape=(
            jax.ShapeDtypeStruct(out.shape, BF16),
            jax.ShapeDtypeStruct(weight_grad.shape, BF16),
        ),
        in_specs=[ANY] * 2,
        out_specs=(ANY, ANY),
        scratch_shapes=[dma((2,))],
        compiler_params=pltpu.CompilerParams(vmem_limit_bytes=4 << 20),
        name="deliver",
    )(out, weight_grad)
    return (out.reshape((1,) + out.shape), weight_grad)


def solution(mesh):
    in_specs = (P("tm", "height", None, None), P(), P(), P(), P("tm", "height", None, None))
    out_specs = (P("tm", None, "height", None), P("height", None))
    return jax.shard_map(local, mesh=mesh, in_specs=in_specs, out_specs=out_specs, check_vma=False)
```

```python
import functools
import math

import jax
import jax.numpy as jnp
from jax import lax
from jax.experimental import pallas as pl
from jax.experimental.pallas import tpu as pltpu
from jax.sharding import PartitionSpec as P

GROUPS = 32
MARGIN = 16
SENT_BY = (0, 0, 0, 0, 0, 0, 1, 2, 3, 4, 3, 4, 5)
KT = 3
MESH = pl.DeviceIdType.MESH
ANY = pl.BlockSpec(memory_space=pl.ANY)
VMEM = pl.BlockSpec(memory_space=pltpu.VMEM)
BF16 = jnp.bfloat16
F32 = jnp.float32


def group_total(row, per_group):
    lane = lax.broadcasted_iota(jnp.int32, row.shape, 1)
    count = row.shape[1]
    span = 1
    while span < per_group:
        low = (lane % (2 * span)) < span
        row = row + jnp.where(low, pltpu.roll(row, count - span, 1), pltpu.roll(row, span, 1))
        span *= 2
    return row


def index_of(inner, a, b, core):
    return (a * inner + b) * 2 + core


def taken(ref, sem):
    pltpu.make_async_copy(ref, ref, sem).wait()


class Stream:
    def __init__(self, dims, place, rows_first, refs, sems):
        self.dims, self.place, self.rows_first = dims, place, rows_first
        self.grad, self.got1, self.sum1, self.got2, self.sum2, self.got3, self.sum3, self.got4, self.part, self.final = refs
        self.send_sem, self.recv_sem = sems
        self.step = 0

    def begin(self, copies):
        for src, dst, to in copies:
            pltpu.make_async_remote_copy(
                src_ref=src,
                dst_ref=dst,
                send_sem=self.send_sem.at[self.step],
                recv_sem=self.recv_sem.at[self.step],
                device_id=to,
                device_id_type=MESH,
            ).start()
        self.step += 1

    def over_rows(self, source, target):
        n_time, n_rows, outer, inner = self.dims
        time, height, a, b, core = self.place
        copies = []
        for step in range(1, inner):
            b_ = (b + step) % inner
            copies.append((source(b_), target.at[step - 1], (time, index_of(inner, a, b_, core))))
        self.begin(copies)

    def over_time(self, source, target):
        n_time, n_rows, outer, inner = self.dims
        time, height, a, b, core = self.place
        copies = []
        for step in range(1, n_time):
            t_ = (time + step) % n_time
            copies.append((source(t_), target.at[step - 1], (t_, height)))
        self.begin(copies)

    def start_pair(self):
        n_time, n_rows, outer, inner = self.dims
        time, height, a, b, core = self.place
        self.begin([(self.grad.at[1 - core], self.got1, (time, index_of(inner, a, b, 1 - core)))])

    def paired(self, t, b_, a_):
        return self.grad[self.place[4], t, b_, a_].astype(F32) + self.got1[t, b_, a_].astype(F32)

    def start_second(self):
        n_time, n_rows, outer, inner = self.dims
        taken(self.got1, self.recv_sem.at[0])
        for t in range(n_time):
            for b_ in range(inner):
                for a_ in range(outer):
                    self.sum1[t, b_, a_] = self.paired(t, b_, a_).astype(BF16)
        if self.rows_first:
            self.over_rows(lambda b_: self.sum1.at[:, b_], self.got2)
        else:
            self.over_time(lambda t_: self.sum1.at[t_], self.got2)

    def start_third(self):
        n_time, n_rows, outer, inner = self.dims
        time, height, a, b, core = self.place
        taken(self.got2, self.recv_sem.at[1])
        for i in range(n_time if self.rows_first else inner):
            for a_ in range(outer):
                total = self.paired(i, b, a_) if self.rows_first else self.paired(time, i, a_)
                for slot in range(self.got2.shape[0]):
                    total = total + self.got2[slot, i, a_].astype(F32)
                self.sum2[i, a_] = total.astype(BF16)
        if self.rows_first:
            self.over_time(lambda t_: self.sum2.at[t_], self.got3)
        else:
            self.over_rows(lambda b_: self.sum2.at[b_], self.got3)

    def start_fourth(self):
        n_time, n_rows, outer, inner = self.dims
        time, height, a, b, core = self.place
        taken(self.got3, self.recv_sem.at[2])
        mine = time if self.rows_first else b
        for a_ in range(outer):
            total = self.sum2[mine, a_].astype(F32)
            for slot in range(self.got3.shape[0]):
                total = total + self.got3[slot, a_].astype(F32)
            self.sum3[a_] = total.astype(BF16)
        copies = []
        for step in range(1, outer):
            a_ = (a + step) % outer
            copies.append((self.sum3.at[a_], self.got4.at[step - 1], (time, index_of(inner, a_, b, core))))
        self.begin(copies)

    def start_last(self, factor):
        n_time, n_rows, outer, inner = self.dims
        time, height, a, b, core = self.place
        taken(self.got4, self.recv_sem.at[3])
        total = self.sum3[a].astype(F32)
        for step in range(1, outer):
            total = total + self.got4[step - 1].astype(F32)
        self.part[...] = (total * factor).astype(BF16)
        self.final[time] = self.part[...]
        self.begin([(self.part, self.final.at[time], ((time + step) % n_time, height)) for step in range(1, n_time)])

    def finish(self):
        n_time = self.dims[0]
        others = self.final.at[pl.ds(0, n_time - 1)]
        taken(others, self.recv_sem.at[4])
        whole = jnp.concatenate([self.final[t] for t in range(n_time)], axis=1)
        for step, ref in enumerate((self.got1, self.got2, self.got3, self.got4, others)):
            taken(ref, self.send_sem.at[step])
        return whole


def block_kernel(dims, cut, factor, act, gain_in, bias_in, weight_in, cot_in, out, wgrad, *scratch):
    n_time, n_rows, outer, inner = dims
    full, taps, alone, gain, bias, weight, cot, cot_next, cot_t, next_t, mine, stats, pooled = scratch[:13]
    local_sem, halo_send, halo_recv, stat_sem, block_sem = scratch[13:18]
    time, height = lax.axis_index("tm"), lax.axis_index("height")
    frames, rows, width, channels = act.shape
    n_out = weight.shape[1]
    own_rows = n_out // n_rows
    pixels = rows * width
    half, edge = width // 2, width // 2 + MARGIN
    area = rows * half
    band = KT * KT * channels
    n_dev = n_time * n_rows
    me = time * n_rows + height
    core, q = height % 2, height // 2
    place = (time, height, q // inner, q % inner, core)
    late_a, late_b, early = (
        Stream(dims, place, rows_first, scratch[i : i + 10], scratch[i + 10 : i + 12])
        for i, rows_first in ((18, True), (30, False), (42, True))
    )
    parts = [(late_b, 0, cut), (late_a, cut, 2 * band), (early, 2 * band, 3 * band)]
    has_up, has_down = height > 0, height < n_rows - 1
    has_next, has_prev = time < n_time - 1, time > 0

    own_frames, old_frames = pl.ds(frames, frames), pl.ds(0, frames)
    loads = [
        pltpu.make_async_copy(act, full.at[own_frames, pl.ds(1, rows)], local_sem.at[0]),
        pltpu.make_async_copy(gain_in, gain, local_sem.at[1]),
        pltpu.make_async_copy(bias_in, bias, local_sem.at[2]),
        pltpu.make_async_copy(cot_in, cot, local_sem.at[3]),
        pltpu.make_async_copy(weight_in, weight, local_sem.at[4]),
    ]
    for load in loads:
        load.start()

    barrier = pltpu.get_barrier_semaphore()
    away_from = 2 * (2 * height // n_rows) - 1

    def peer(step):
        return (time + step // n_rows) % n_time, (height + n_rows + away_from * (step % n_rows)) % n_rows

    def greet(step, carry):
        pl.semaphore_signal(barrier, inc=1, device_id=peer(step), device_id_type=MESH)
        return carry

    for lag in range(1, n_time):
        lax.fori_loop(lag * n_rows + 1, (lag + 1) * n_rows, greet, 0)
        greet(lag * n_rows, 0)
    lax.fori_loop(1, n_rows, greet, 0)

    loads[0].wait()
    local = frames * pixels
    chan_sum = jnp.zeros((1, channels), F32)
    for f in range(frames):
        for r in range(rows):
            chan_sum = chan_sum + jnp.sum(full[frames + f, 1 + r].astype(F32), axis=0, keepdims=True)
    chan_mean = chan_sum * (1.0 / local)
    chan_dev = jnp.zeros((1, channels), F32)
    for f in range(frames):
        for r in range(rows):
            away = full[frames + f, 1 + r].astype(F32) - chan_mean
            chan_dev = chan_dev + jnp.sum(away * away, axis=0, keepdims=True)
    packed = jnp.concatenate([chan_mean, chan_dev], axis=0)
    mine[...] = packed
    stats[me] = packed
    loads[3].wait()
    with jax.named_scope("entry"):
        pl.semaphore_wait(barrier, n_dev - 1)

    def send(step, carry):
        pltpu.make_async_remote_copy(
            src_ref=mine,
            dst_ref=stats.at[me],
            send_sem=stat_sem.at[0],
            recv_sem=stat_sem.at[1],
            device_id=peer(step),
            device_id_type=MESH,
        ).start()
        return carry

    def own_to_old(row, count, begin, end):
        place_in = (pl.ds(row, count), pl.ds(begin, end - begin))
        return full.at[own_frames, *place_in], full.at[old_frames, *place_in]

    def relay(row, to_row, begin, end):
        columns = pl.ds(begin, end - begin)
        return full.at[old_frames, pl.ds(row, 1), columns], full.at[old_frames, pl.ds(to_row, 1), columns]

    moves = [
        (*own_to_old(rows, 1, 0, edge), 1, 0, has_next, has_prev),
        (*own_to_old(1, 1, 0, edge), 1, 0, has_next, has_prev),
        (*own_to_old(2, rows - 2, 0, edge), 1, 0, has_next, has_prev),
        (*own_to_old(rows, 1, edge, width), 1, 0, has_next, has_prev),
        (*own_to_old(1, 1, edge, width), 1, 0, has_next, has_prev),
        (*own_to_old(2, rows - 2, edge, width), 1, 0, has_next, has_prev),
        (full.at[own_frames, pl.ds(1, 1)], full.at[own_frames, pl.ds(rows + 1, 1)], 0, -1, has_up, has_down),
        (full.at[own_frames, pl.ds(rows, 1)], full.at[own_frames, pl.ds(0, 1)], 0, 1, has_down, has_up),
        (*relay(rows, 0, 0, edge), 0, 1, has_prev & has_down, has_prev & has_up),
        (*relay(1, rows + 1, 0, edge), 0, -1, has_prev & has_up, has_prev & has_down),
        (*relay(rows, 0, edge, width), 0, 1, has_prev & has_down, has_prev & has_up),
        (*relay(1, rows + 1, edge, width), 0, -1, has_prev & has_up, has_prev & has_down),
        (cot.at[:, pl.ds(half, half)], cot_next, -1, 0, has_prev, has_next),
    ]

    def halo(index):
        source, target, frame_step, row_step = moves[index][:4]
        return pltpu.make_async_remote_copy(
            src_ref=source,
            dst_ref=target,
            send_sem=halo_send.at[SENT_BY[index]],
            recv_sem=halo_recv.at[index],
            device_id=(time + frame_step, height + row_step),
            device_id_type=MESH,
        )

    def start(index):
        pl.when(moves[index][4])(lambda: halo(index).start())

    def arrived(index):
        pl.when(moves[index][5])(lambda: halo(index).wait_recv())

    with jax.named_scope("sends"):
        for lag in range(1, n_time):
            lax.fori_loop(lag * n_rows + 1, (lag + 1) * n_rows, send, 0)
            send(lag * n_rows, 0)
        for index in (0, 1, 12, 2, 3, 4, 5):
            start(index)
        lax.fori_loop(1, n_rows, send, 0)
        for index in (6, 7):
            start(index)

    zero_rows = jnp.zeros((2 * frames, 1, width, channels), BF16)

    @pl.when(jnp.logical_not(has_up))
    def _():
        full[:, pl.ds(0, 1)] = zero_rows

    @pl.when(jnp.logical_not(has_down))
    def _():
        full[:, pl.ds(rows + 1, 1)] = zero_rows

    for y in range(rows):
        turned = cot[y].astype(F32).T.astype(BF16)
        for side in range(2):
            cot_t[:, side * area + y * half : side * area + (y + 1) * half] = turned[:, side * half : (side + 1) * half]
    for index in (1, 2, 4):
        loads[index].wait()

    with jax.named_scope("halo_relay"):
        arrived(0)
        start(8)
    with jax.named_scope("stats_in"):
        taken(stats.at[pl.ds(0, n_dev - 1)], stat_sem.at[1])
    per_group = channels // GROUPS
    means, devs = stats[:, 0], stats[:, 1]
    mean = group_total(jnp.sum(means, axis=0, keepdims=True), per_group) * (1.0 / (n_dev * per_group))
    away = means - mean
    spread = jnp.sum(devs + local * (away * away), axis=0, keepdims=True)
    var = group_total(spread, per_group) * (1.0 / (local * n_dev * per_group))
    scale = lax.rsqrt(var + 1e-06) * gain[...]
    shift = bias[...]
    column = lax.broadcasted_iota(jnp.int32, (edge, channels), 0)

    def normed(f, r, side):
        inside = jnp.logical_and(r + height > 0, r + height * rows < n_rows * rows + 1)
        v = (full[f, r, side * (width - edge) : side * (width - edge) + edge].astype(F32) - mean) * scale + shift
        v = v / (1.0 + jnp.exp(-v))
        return v.astype(BF16).astype(F32) * inside.astype(F32)

    def line(r):
        return pl.ds(pl.multiple_of(r * half, half), half)

    def put(t, side, r, value):
        left, right = pltpu.roll(value, 1, 0), pltpu.roll(value, edge - 1, 0)
        if side == 0:
            left = jnp.where(column == 0, 0.0, left)
        else:
            right = jnp.where(column == edge - 1, 0.0, right)
        for c, part in enumerate((left, value, right)):
            taps[t, side, line(r), c * channels : (c + 1) * channels] = part[
                side * MARGIN : side * MARGIN + half
            ].astype(BF16)

    OLD, MIXED, OWN, ONE, TWO = range(5)

    def prepare_own(r, carry):
        for side in range(2):
            one, two = normed(frames, r, side), normed(frames + 1, r, side)
            put(OWN, side, r, one + two)
            put(ONE, side, r, one)
            put(TWO, side, r, two)
        return carry

    def prepare_old(side):
        def body(r, carry):
            one, two = normed(0, r, side), normed(1, r, side)
            put(OLD, side, r, one + two)
            put(MIXED, side, r, two + normed(frames, r, side))
            return carry

        @pl.when(has_prev)
        def _():
            lax.fori_loop(0, rows + 2, body, 0)

    def repeat_first(r, carry):
        for side in range(2):
            twice = (taps[ONE, side, line(r), :].astype(F32) * 2.0).astype(BF16)
            taps[OLD, side, line(r), :] = twice
            taps[MIXED, side, line(r), :] = twice
        return carry

    with jax.named_scope("prep_own"):
        lax.fori_loop(1, rows + 1, prepare_own, 0)
    with jax.named_scope("halo_own"):
        arrived(6)
        arrived(7)
    with jax.named_scope("prep_own_edge"):
        lax.fori_loop(0, 2, lambda i, carry: prepare_own(i * (rows + 1), carry), 0)

    def windows(t, side):
        return [taps[t, side, r * half : r * half + area] for r in range(KT)]

    def gradient(lhs, t, side):
        return jnp.dot(lhs, jnp.concatenate(windows(t, side), axis=1), preferred_element_type=F32)

    left_t, right_t = cot_t.at[:, pl.ds(0, area)], cot_t.at[:, pl.ds(area, area)]

    def store(t, total):
        total = total.astype(BF16)
        for stream, first, last in parts:
            span = stream.grad.shape[-1]
            for piece in range(n_time):
                lead = first + piece * span
                begin, end = max(lead, t * band), min(lead + span, last, (t + 1) * band)
                if begin < end:
                    part = total[:, begin - t * band : end - t * band]
                    for block in range(n_rows):
                        q_, core_ = block // 2, block % 2
                        stream.grad[core_, piece, q_ % inner, q_ // inner, :, begin - lead : end - lead] = part[
                            block * own_rows : (block + 1) * own_rows
                        ]
                unused = max(last, lead) - lead
                if unused < span and (last - 1) // band == t:
                    stream.grad[:, piece, :, :, :, unused:] = jnp.zeros(
                        (2, inner, outer, own_rows, span - unused), BF16
                    )

    def conv(side):
        lhs = jnp.concatenate([piece for t in (OLD, MIXED, OWN) for piece in windows(t, side)], axis=1)
        total = jnp.dot(lhs, weight[...], preferred_element_type=F32) * 0.5
        for y in range(rows):
            part = total[y * half : (y + 1) * half].T.astype(BF16)
            pooled[:, y, :, side * half : (side + 1) * half] = part.reshape(n_rows, own_rows, half)

    def spread_out(side, crossing):
        columns = pl.ds(side * half, half)
        for cross in range(1, inner) if crossing else [0]:
            for lag in range(outer):
                for core_ in range(2):
                    if cross or lag or core_:
                        other = index_of(
                            inner, (place[2] + lag) % outer, (place[3] + cross) % inner, (core + core_) % 2
                        )
                        pltpu.make_async_remote_copy(
                            src_ref=pooled.at[other, :, :, columns],
                            dst_ref=out.at[pl.ds(height * rows, rows), :, columns],
                            send_sem=block_sem.at[0],
                            recv_sem=block_sem.at[1],
                            device_id=(time, other),
                            device_id_type=MESH,
                        ).start()

    @pl.when(jnp.logical_not(has_prev))
    def _():
        with jax.named_scope("repeat_first"):
            lax.fori_loop(0, rows + 2, repeat_first, 0)

    with jax.named_scope("halo_relay2"):
        arrived(1)
        start(9)
    with jax.named_scope("grad_own"):
        store(2, gradient(left_t[...], OWN, 0) + gradient(right_t[...], OWN, 1))
        early.start_pair()
    with jax.named_scope("grad_alone"):
        alone[...] = gradient(right_t[...], ONE, 1)

    @pl.when(jnp.logical_not(has_prev))
    def _():
        with jax.named_scope("conv_first_a"):
            conv(0)

    with jax.named_scope("early2"):
        early.start_second()

    @pl.when(jnp.logical_not(has_prev))
    def _():
        spread_out(0, False)

    with jax.named_scope("cot_next"):
        arrived(12)

        @pl.when(has_next)
        def _():
            for y in range(rows):
                next_t[:, y * half : (y + 1) * half] = cot_next[y].astype(F32).T.astype(BF16)

    with jax.named_scope("halo_old_a"):
        for index in (2, 8, 9):
            arrived(index)
    with jax.named_scope("prep_old_a"):
        prepare_old(0)

    once = jnp.where(has_prev, 1.0, 2.0).astype(F32)
    extra = jnp.where(has_prev, 0.0, 2.0).astype(F32)

    def late_term(t, factor_alone, next_t_of):
        total = alone[...] * factor_alone + gradient(left_t[...], t, 0)

        @pl.when(has_next)
        def _():
            store(t, total + gradient(next_t[...], next_t_of, 1))

        @pl.when(jnp.logical_not(has_next))
        def _():
            store(t, total)

    with jax.named_scope("grad_late"):
        late_term(MIXED, once, TWO)
        late_term(OLD, extra, OWN)
        late_b.start_pair()
        late_a.start_pair()
    with jax.named_scope("halo_relay3"):
        arrived(3)
        start(10)

    with jax.named_scope("conv_1st"):

        @pl.when(has_prev)
        def _():
            conv(0)
            arrived(4)
            start(11)
            spread_out(0, False)

        @pl.when(jnp.logical_not(has_prev))
        def _():
            conv(1)
            spread_out(1, False)

    with jax.named_scope("late2"):
        late_b.start_second()
        late_a.start_second()
    with jax.named_scope("early3"):
        early.start_third()
    with jax.named_scope("halo_old_b"):
        for index in (5, 10, 11):
            arrived(index)
    with jax.named_scope("prep_old_b"):
        prepare_old(1)

    @pl.when(has_prev)
    def _():
        with jax.named_scope("conv_b"):
            conv(1)
            spread_out(1, False)

    out[pl.ds(height * rows, rows)] = pooled[height]
    with jax.named_scope("late3a"):
        late_a.start_third()
    with jax.named_scope("late3b"):
        late_b.start_third()
    with jax.named_scope("early4"):
        early.start_fourth()
    with jax.named_scope("late4a"):
        late_a.start_fourth()
    with jax.named_scope("late4b"):
        late_b.start_fourth()
    with jax.named_scope("last"):
        early.start_last(factor)
        spread_out(0, True)
        spread_out(1, True)
        late_a.start_last(factor)
        late_b.start_last(factor)
    with jax.named_scope("finish"):
        for stream, first, last in parts:
            wgrad[:, first:last] = stream.finish()[:, : last - first]

    with jax.named_scope("blocks_in"):
        taken(out.at[pl.ds(0, (n_rows - 1) * rows)], block_sem.at[1])
    with jax.named_scope("sent"):
        taken(out.at[pl.ds(0, (n_rows - 1) * rows)], block_sem.at[0])
        taken(stats.at[pl.ds(0, n_dev - 1)], stat_sem.at[0])
        border = full.at[own_frames, pl.ds(0, 1)]
        whole = [full.at[own_frames, pl.ds(1, rows)], border, border, border, border, cot_next]
        for index, ref in enumerate(whole):
            first = moves[SENT_BY.index(index)]
            pl.when(first[4])(functools.partial(taken, ref, halo_send.at[index]))


def deliver_kernel(block_in, grad_in, block_out, grad_out, sem):
    copies = [
        pltpu.make_async_copy(block_in, block_out, sem.at[0]),
        pltpu.make_async_copy(grad_in, grad_out, sem.at[1]),
    ]
    for copy in copies:
        copy.start()
    for copy in copies:
        copy.wait()


def local(activations, norm_gain, norm_bias, conv_weight, cotangent):
    frames, rows, width, channels = activations.shape
    depth, n_out = conv_weight.shape
    n_time, n_rows = lax.axis_size("tm"), lax.axis_size("height")
    n_dev = n_time * n_rows
    inner = 2
    outer = n_rows // (2 * inner)
    own_rows = n_out // n_rows
    dims = (n_time, n_rows, outer, inner)
    dma = pltpu.SemaphoreType.DMA
    factor = 0.5 / math.sqrt(frames * n_time * rows * n_rows * width)

    def stream(length, rows_first):
        span = -(-length // (128 * n_time)) * 128
        steps = [n_time, inner] if rows_first else [inner, n_time]
        chunk = (outer, own_rows, span)
        shapes = [
            (2, n_time, inner, *chunk),
            (n_time, inner, *chunk),
            (n_time, inner, *chunk),
            (steps[1] - 1, steps[0], *chunk),
            (steps[0], *chunk),
            (steps[0] - 1, *chunk),
            chunk,
            (outer - 1, own_rows, span),
            (own_rows, span),
            (n_time, own_rows, span),
        ]
        return [pltpu.VMEM(shape, BF16) for shape in shapes] + [dma((5,)), dma((5,))]

    band = depth // KT
    cut = 8 * channels
    out, weight_grad = pl.pallas_call(
        functools.partial(block_kernel, dims, cut, factor),
        out_shape=(
            pltpu.VMEM((rows * n_rows, own_rows, width), BF16),
            pltpu.VMEM((own_rows, depth), BF16),
        ),
        in_specs=[ANY] * 5,
        out_specs=(VMEM, VMEM),
        scratch_shapes=[
            pltpu.VMEM((2 * frames, rows + 2, width, channels), BF16),
            pltpu.VMEM((5, 2, (rows + 2) * (width // 2), KT * channels), BF16),
            pltpu.VMEM((n_out, band), F32),
            pltpu.VMEM((1, channels), F32),
            pltpu.VMEM((1, channels), F32),
            pltpu.VMEM((depth, n_out), BF16),
            pltpu.VMEM((rows, width, n_out), BF16),
            pltpu.VMEM((rows, width // 2, n_out), BF16),
            pltpu.VMEM((n_out, rows * width), BF16),
            pltpu.VMEM((n_out, rows * (width // 2)), BF16),
            pltpu.VMEM((2, channels), F32),
            pltpu.VMEM((n_dev, 2, channels), F32),
            pltpu.VMEM((n_rows, rows, own_rows, width), BF16),
            dma((5,)),
            dma((6,)),
            dma((13,)),
            dma((2,)),
            dma((2,)),
            *stream(2 * band - cut, True),
            *stream(cut, False),
            *stream(band, True),
        ],
        compiler_params=pltpu.CompilerParams(collective_id=0, has_side_effects=True, vmem_limit_bytes=60 << 20),
        name="block",
    )(
        activations,
        norm_gain.reshape(1, channels),
        norm_bias.reshape(1, channels),
        conv_weight,
        cotangent.reshape(rows, width, n_out),
    )
    out, weight_grad = pl.pallas_call(
        deliver_kernel,
        out_shape=(
            jax.ShapeDtypeStruct(out.shape, BF16),
            jax.ShapeDtypeStruct(weight_grad.shape, BF16),
        ),
        in_specs=[ANY] * 2,
        out_specs=(ANY, ANY),
        scratch_shapes=[dma((2,))],
        compiler_params=pltpu.CompilerParams(vmem_limit_bytes=4 << 20),
        name="deliver",
    )(out, weight_grad)
    return (out.reshape((1,) + out.shape), weight_grad)


def solution(mesh):
    in_specs = (P("tm", "height", None, None), P(), P(), P(), P("tm", "height", None, None))
    out_specs = (P("tm", None, "height", None), P("height", None))
    return jax.shard_map(local, mesh=mesh, in_specs=in_specs, out_specs=out_specs, check_vma=False)
```

```python
import functools
import math

import jax
import jax.numpy as jnp
from jax import lax
from jax.experimental import pallas as pl
from jax.experimental.pallas import tpu as pltpu
from jax.sharding import PartitionSpec as P

GROUPS = 32
MARGIN = 16
SENT_BY = (0, 0, 0, 0, 0, 0, 1, 2, 3, 4, 3, 4, 5)
KT = 3
MESH = pl.DeviceIdType.MESH
ANY = pl.BlockSpec(memory_space=pl.ANY)
VMEM = pl.BlockSpec(memory_space=pltpu.VMEM)
BF16 = jnp.bfloat16
F32 = jnp.float32


def group_total(row, per_group):
    lane = lax.broadcasted_iota(jnp.int32, row.shape, 1)
    count = row.shape[1]
    span = 1
    while span < per_group:
        low = (lane % (2 * span)) < span
        row = row + jnp.where(low, pltpu.roll(row, count - span, 1), pltpu.roll(row, span, 1))
        span *= 2
    return row


def index_of(inner, a, b, core):
    return (a * inner + b) * 2 + core


def taken(ref, sem):
    pltpu.make_async_copy(ref, ref, sem).wait()


class Stream:
    def __init__(self, dims, place, rows_first, refs, sems):
        self.dims, self.place, self.rows_first = dims, place, rows_first
        self.grad, self.got1, self.sum1, self.got2, self.sum2, self.got3, self.sum3, self.got4, self.part, self.final = refs
        self.send_sem, self.recv_sem = sems
        self.step = 0

    def begin(self, copies):
        for src, dst, to in copies:
            pltpu.make_async_remote_copy(
                src_ref=src,
                dst_ref=dst,
                send_sem=self.send_sem.at[self.step],
                recv_sem=self.recv_sem.at[self.step],
                device_id=to,
                device_id_type=MESH,
            ).start()
        self.step += 1

    def over_rows(self, source, target):
        n_time, n_rows, outer, inner = self.dims
        time, height, a, b, core = self.place
        copies = []
        for step in range(1, inner):
            b_ = (b + step) % inner
            copies.append((source(b_), target.at[step - 1], (time, index_of(inner, a, b_, core))))
        self.begin(copies)

    def over_time(self, source, target):
        n_time, n_rows, outer, inner = self.dims
        time, height, a, b, core = self.place
        copies = []
        for step in range(1, n_time):
            t_ = (time + step) % n_time
            copies.append((source(t_), target.at[step - 1], (t_, height)))
        self.begin(copies)

    def start_pair(self):
        n_time, n_rows, outer, inner = self.dims
        time, height, a, b, core = self.place
        self.begin([(self.grad.at[1 - core], self.got1, (time, index_of(inner, a, b, 1 - core)))])

    def paired(self, t, b_, a_):
        return self.grad[self.place[4], t, b_, a_].astype(F32) + self.got1[t, b_, a_].astype(F32)

    def start_second(self):
        n_time, n_rows, outer, inner = self.dims
        taken(self.got1, self.recv_sem.at[0])
        for t in range(n_time):
            for b_ in range(inner):
                for a_ in range(outer):
                    self.sum1[t, b_, a_] = self.paired(t, b_, a_).astype(BF16)
        if self.rows_first:
            self.over_rows(lambda b_: self.sum1.at[:, b_], self.got2)
        else:
            self.over_time(lambda t_: self.sum1.at[t_], self.got2)

    def start_third(self):
        n_time, n_rows, outer, inner = self.dims
        time, height, a, b, core = self.place
        taken(self.got2, self.recv_sem.at[1])
        for i in range(n_time if self.rows_first else inner):
            for a_ in range(outer):
                total = self.paired(i, b, a_) if self.rows_first else self.paired(time, i, a_)
                for slot in range(self.got2.shape[0]):
                    total = total + self.got2[slot, i, a_].astype(F32)
                self.sum2[i, a_] = total.astype(BF16)
        if self.rows_first:
            self.over_time(lambda t_: self.sum2.at[t_], self.got3)
        else:
            self.over_rows(lambda b_: self.sum2.at[b_], self.got3)

    def start_fourth(self):
        n_time, n_rows, outer, inner = self.dims
        time, height, a, b, core = self.place
        taken(self.got3, self.recv_sem.at[2])
        mine = time if self.rows_first else b
        for a_ in range(outer):
            total = self.sum2[mine, a_].astype(F32)
            for slot in range(self.got3.shape[0]):
                total = total + self.got3[slot, a_].astype(F32)
            self.sum3[a_] = total.astype(BF16)
        copies = []
        for step in range(1, outer):
            a_ = (a + step) % outer
            copies.append((self.sum3.at[a_], self.got4.at[step - 1], (time, index_of(inner, a_, b, core))))
        self.begin(copies)

    def start_last(self, factor):
        n_time, n_rows, outer, inner = self.dims
        time, height, a, b, core = self.place
        taken(self.got4, self.recv_sem.at[3])
        total = self.sum3[a].astype(F32)
        for step in range(1, outer):
            total = total + self.got4[step - 1].astype(F32)
        self.part[...] = (total * factor).astype(BF16)
        self.final[time] = self.part[...]
        self.begin([(self.part, self.final.at[time], ((time + step) % n_time, height)) for step in range(1, n_time)])

    def finish(self):
        n_time = self.dims[0]
        others = self.final.at[pl.ds(0, n_time - 1)]
        taken(others, self.recv_sem.at[4])
        whole = jnp.concatenate([self.final[t] for t in range(n_time)], axis=1)
        for step, ref in enumerate((self.got1, self.got2, self.got3, self.got4, others)):
            taken(ref, self.send_sem.at[step])
        return whole


def block_kernel(dims, cut, factor, act, gain_in, bias_in, weight_in, cot_in, out, wgrad, *scratch):
    n_time, n_rows, outer, inner = dims
    full, taps, alone, gain, bias, weight, cot, cot_next, cot_t, next_t, mine, stats, pooled = scratch[:13]
    local_sem, halo_send, halo_recv, stat_sem, block_sem = scratch[13:18]
    time, height = lax.axis_index("tm"), lax.axis_index("height")
    frames, rows, width, channels = act.shape
    n_out = weight.shape[1]
    own_rows = n_out // n_rows
    pixels = rows * width
    half, edge = width // 2, width // 2 + MARGIN
    area = rows * half
    band = KT * KT * channels
    n_dev = n_time * n_rows
    me = time * n_rows + height
    core, q = height % 2, height // 2
    place = (time, height, q // inner, q % inner, core)
    late_a, late_b, early = (
        Stream(dims, place, rows_first, scratch[i : i + 10], scratch[i + 10 : i + 12])
        for i, rows_first in ((18, True), (30, False), (42, True))
    )
    parts = [(late_b, 0, cut), (late_a, cut, 2 * band), (early, 2 * band, 3 * band)]
    has_up, has_down = height > 0, height < n_rows - 1
    has_next, has_prev = time < n_time - 1, time > 0

    own_frames, old_frames = pl.ds(frames, frames), pl.ds(0, frames)
    loads = [
        pltpu.make_async_copy(act, full.at[own_frames, pl.ds(1, rows)], local_sem.at[0]),
        pltpu.make_async_copy(gain_in, gain, local_sem.at[1]),
        pltpu.make_async_copy(bias_in, bias, local_sem.at[2]),
        pltpu.make_async_copy(cot_in, cot, local_sem.at[3]),
        pltpu.make_async_copy(weight_in, weight, local_sem.at[4]),
    ]
    for load in loads:
        load.start()

    barrier = pltpu.get_barrier_semaphore()
    away_from = 2 * (2 * height // n_rows) - 1

    def peer(step):
        return (time + step // n_rows) % n_time, (height + n_rows + away_from * (step % n_rows)) % n_rows

    def greet(step, carry):
        pl.semaphore_signal(barrier, inc=1, device_id=peer(step), device_id_type=MESH)
        return carry

    for lag in range(1, n_time):
        lax.fori_loop(lag * n_rows + 1, (lag + 1) * n_rows, greet, 0, unroll=5)
        greet(lag * n_rows, 0)
    lax.fori_loop(1, n_rows, greet, 0, unroll=5)

    loads[0].wait()
    local = frames * pixels
    chan_sum = jnp.zeros((1, channels), F32)
    for f in range(frames):
        for r in range(rows):
            chan_sum = chan_sum + jnp.sum(full[frames + f, 1 + r].astype(F32), axis=0, keepdims=True)
    chan_mean = chan_sum * (1.0 / local)
    chan_dev = jnp.zeros((1, channels), F32)
    for f in range(frames):
        for r in range(rows):
            away = full[frames + f, 1 + r].astype(F32) - chan_mean
            chan_dev = chan_dev + jnp.sum(away * away, axis=0, keepdims=True)
    packed = jnp.concatenate([chan_mean, chan_dev], axis=0)
    mine[...] = packed
    stats[me] = packed
    loads[3].wait()
    with jax.named_scope("entry"):
        pl.semaphore_wait(barrier, n_dev - 1)

    def send(step, carry):
        pltpu.make_async_remote_copy(
            src_ref=mine,
            dst_ref=stats.at[me],
            send_sem=stat_sem.at[0],
            recv_sem=stat_sem.at[1],
            device_id=peer(step),
            device_id_type=MESH,
        ).start()
        return carry

    def own_to_old(row, count, begin, end):
        place_in = (pl.ds(row, count), pl.ds(begin, end - begin))
        return full.at[own_frames, *place_in], full.at[old_frames, *place_in]

    def relay(row, to_row, begin, end):
        columns = pl.ds(begin, end - begin)
        return full.at[old_frames, pl.ds(row, 1), columns], full.at[old_frames, pl.ds(to_row, 1), columns]

    moves = [
        (*own_to_old(rows, 1, 0, edge), 1, 0, has_next, has_prev),
        (*own_to_old(1, 1, 0, edge), 1, 0, has_next, has_prev),
        (*own_to_old(2, rows - 2, 0, edge), 1, 0, has_next, has_prev),
        (*own_to_old(rows, 1, edge, width), 1, 0, has_next, has_prev),
        (*own_to_old(1, 1, edge, width), 1, 0, has_next, has_prev),
        (*own_to_old(2, rows - 2, edge, width), 1, 0, has_next, has_prev),
        (full.at[own_frames, pl.ds(1, 1)], full.at[own_frames, pl.ds(rows + 1, 1)], 0, -1, has_up, has_down),
        (full.at[own_frames, pl.ds(rows, 1)], full.at[own_frames, pl.ds(0, 1)], 0, 1, has_down, has_up),
        (*relay(rows, 0, 0, edge), 0, 1, has_prev & has_down, has_prev & has_up),
        (*relay(1, rows + 1, 0, edge), 0, -1, has_prev & has_up, has_prev & has_down),
        (*relay(rows, 0, edge, width), 0, 1, has_prev & has_down, has_prev & has_up),
        (*relay(1, rows + 1, edge, width), 0, -1, has_prev & has_up, has_prev & has_down),
        (cot.at[:, pl.ds(half, half)], cot_next, -1, 0, has_prev, has_next),
    ]

    def halo(index):
        source, target, frame_step, row_step = moves[index][:4]
        return pltpu.make_async_remote_copy(
            src_ref=source,
            dst_ref=target,
            send_sem=halo_send.at[SENT_BY[index]],
            recv_sem=halo_recv.at[index],
            device_id=(time + frame_step, height + row_step),
            device_id_type=MESH,
        )

    def start(index):
        pl.when(moves[index][4])(lambda: halo(index).start())

    def arrived(index):
        pl.when(moves[index][5])(lambda: halo(index).wait_recv())

    with jax.named_scope("sends"):
        for lag in range(1, n_time):
            lax.fori_loop(lag * n_rows + 1, (lag + 1) * n_rows, send, 0, unroll=5)
            send(lag * n_rows, 0)
        for index in (0, 1, 12, 2, 3, 4, 5):
            start(index)
        lax.fori_loop(1, n_rows, send, 0, unroll=5)
        for index in (6, 7):
            start(index)

    zero_rows = jnp.zeros((2 * frames, 1, width, channels), BF16)

    @pl.when(jnp.logical_not(has_up))
    def _():
        full[:, pl.ds(0, 1)] = zero_rows

    @pl.when(jnp.logical_not(has_down))
    def _():
        full[:, pl.ds(rows + 1, 1)] = zero_rows

    for y in range(rows):
        turned = cot[y].astype(F32).T.astype(BF16)
        for side in range(2):
            cot_t[:, side * area + y * half : side * area + (y + 1) * half] = turned[:, side * half : (side + 1) * half]
    for index in (1, 2, 4):
        loads[index].wait()

    with jax.named_scope("halo_relay"):
        arrived(0)
        start(8)
    with jax.named_scope("stats_in"):
        taken(stats.at[pl.ds(0, n_dev - 1)], stat_sem.at[1])
    per_group = channels // GROUPS
    means, devs = stats[:, 0], stats[:, 1]
    mean = group_total(jnp.sum(means, axis=0, keepdims=True), per_group) * (1.0 / (n_dev * per_group))
    away = means - mean
    spread = jnp.sum(devs + local * (away * away), axis=0, keepdims=True)
    var = group_total(spread, per_group) * (1.0 / (local * n_dev * per_group))
    scale = lax.rsqrt(var + 1e-06) * gain[...]
    shift = bias[...]
    column = lax.broadcasted_iota(jnp.int32, (edge, channels), 0)

    def normed(f, r, side):
        inside = jnp.logical_and(r + height > 0, r + height * rows < n_rows * rows + 1)
        v = (full[f, r, side * (width - edge) : side * (width - edge) + edge].astype(F32) - mean) * scale + shift
        v = v / (1.0 + jnp.exp(-v))
        return v.astype(BF16).astype(F32) * inside.astype(F32)

    def line(r):
        return pl.ds(pl.multiple_of(r * half, half), half)

    def put(t, side, r, value):
        left, right = pltpu.roll(value, 1, 0), pltpu.roll(value, edge - 1, 0)
        if side == 0:
            left = jnp.where(column == 0, 0.0, left)
        else:
            right = jnp.where(column == edge - 1, 0.0, right)
        for c, part in enumerate((left, value, right)):
            taps[t, side, line(r), c * channels : (c + 1) * channels] = part[
                side * MARGIN : side * MARGIN + half
            ].astype(BF16)

    OLD, MIXED, OWN, ONE, TWO = range(5)

    def prepare_own(r, carry):
        for side in range(2):
            one, two = normed(frames, r, side), normed(frames + 1, r, side)
            put(OWN, side, r, one + two)
            put(ONE, side, r, one)
            put(TWO, side, r, two)
        return carry

    def prepare_old(side):
        def body(r, carry):
            one, two = normed(0, r, side), normed(1, r, side)
            put(OLD, side, r, one + two)
            put(MIXED, side, r, two + normed(frames, r, side))
            return carry

        @pl.when(has_prev)
        def _():
            lax.fori_loop(0, rows + 2, body, 0)

    def repeat_first(r, carry):
        for side in range(2):
            twice = (taps[ONE, side, line(r), :].astype(F32) * 2.0).astype(BF16)
            taps[OLD, side, line(r), :] = twice
            taps[MIXED, side, line(r), :] = twice
        return carry

    with jax.named_scope("prep_own"):
        lax.fori_loop(1, rows + 1, prepare_own, 0)
    with jax.named_scope("halo_own"):
        arrived(6)
        arrived(7)
    with jax.named_scope("prep_own_edge"):
        lax.fori_loop(0, 2, lambda i, carry: prepare_own(i * (rows + 1), carry), 0)

    def windows(t, side):
        return [taps[t, side, r * half : r * half + area] for r in range(KT)]

    def gradient(lhs, t, side):
        return jnp.dot(lhs, jnp.concatenate(windows(t, side), axis=1), preferred_element_type=F32)

    left_t, right_t = cot_t.at[:, pl.ds(0, area)], cot_t.at[:, pl.ds(area, area)]

    def store(t, total):
        total = total.astype(BF16)
        for stream, first, last in parts:
            span = stream.grad.shape[-1]
            for piece in range(n_time):
                lead = first + piece * span
                begin, end = max(lead, t * band), min(lead + span, last, (t + 1) * band)
                if begin < end:
                    part = total[:, begin - t * band : end - t * band]
                    for block in range(n_rows):
                        q_, core_ = block // 2, block % 2
                        stream.grad[core_, piece, q_ % inner, q_ // inner, :, begin - lead : end - lead] = part[
                            block * own_rows : (block + 1) * own_rows
                        ]
                unused = max(last, lead) - lead
                if unused < span and (last - 1) // band == t:
                    stream.grad[:, piece, :, :, :, unused:] = jnp.zeros(
                        (2, inner, outer, own_rows, span - unused), BF16
                    )

    def conv(side):
        lhs = jnp.concatenate([piece for t in (OLD, MIXED, OWN) for piece in windows(t, side)], axis=1)
        total = jnp.dot(lhs, weight[...], preferred_element_type=F32) * 0.5
        for y in range(rows):
            part = total[y * half : (y + 1) * half].T.astype(BF16)
            pooled[:, y, :, side * half : (side + 1) * half] = part.reshape(n_rows, own_rows, half)

    def spread_out(side, crossing):
        columns = pl.ds(side * half, half)
        for cross in range(1, inner) if crossing else [0]:
            for lag in range(outer):
                for core_ in range(2):
                    if cross or lag or core_:
                        other = index_of(
                            inner, (place[2] + lag) % outer, (place[3] + cross) % inner, (core + core_) % 2
                        )
                        pltpu.make_async_remote_copy(
                            src_ref=pooled.at[other, :, :, columns],
                            dst_ref=out.at[pl.ds(height * rows, rows), :, columns],
                            send_sem=block_sem.at[0],
                            recv_sem=block_sem.at[1],
                            device_id=(time, other),
                            device_id_type=MESH,
                        ).start()

    @pl.when(jnp.logical_not(has_prev))
    def _():
        with jax.named_scope("repeat_first"):
            lax.fori_loop(0, rows + 2, repeat_first, 0)

    with jax.named_scope("halo_relay2"):
        arrived(1)
        start(9)
    with jax.named_scope("grad_own"):
        store(2, gradient(left_t[...], OWN, 0) + gradient(right_t[...], OWN, 1))
        early.start_pair()
    with jax.named_scope("grad_alone"):
        alone[...] = gradient(right_t[...], ONE, 1)

    @pl.when(jnp.logical_not(has_prev))
    def _():
        with jax.named_scope("conv_first_a"):
            conv(0)

    with jax.named_scope("early2"):
        early.start_second()

    @pl.when(jnp.logical_not(has_prev))
    def _():
        spread_out(0, False)

    with jax.named_scope("cot_next"):
        arrived(12)

        @pl.when(has_next)
        def _():
            for y in range(rows):
                next_t[:, y * half : (y + 1) * half] = cot_next[y].astype(F32).T.astype(BF16)

    with jax.named_scope("halo_old_a"):
        for index in (2, 8, 9):
            arrived(index)
    with jax.named_scope("prep_old_a"):
        prepare_old(0)

    once = jnp.where(has_prev, 1.0, 2.0).astype(F32)
    extra = jnp.where(has_prev, 0.0, 2.0).astype(F32)

    def late_term(t, factor_alone, next_t_of):
        total = alone[...] * factor_alone + gradient(left_t[...], t, 0)

        @pl.when(has_next)
        def _():
            store(t, total + gradient(next_t[...], next_t_of, 1))

        @pl.when(jnp.logical_not(has_next))
        def _():
            store(t, total)

    with jax.named_scope("grad_late"):
        late_term(MIXED, once, TWO)
        late_term(OLD, extra, OWN)
        late_b.start_pair()
        late_a.start_pair()
    with jax.named_scope("halo_relay3"):
        arrived(3)
        start(10)

    with jax.named_scope("conv_1st"):

        @pl.when(has_prev)
        def _():
            conv(0)
            arrived(4)
            start(11)
            spread_out(0, False)

        @pl.when(jnp.logical_not(has_prev))
        def _():
            conv(1)
            spread_out(1, False)

    with jax.named_scope("late2"):
        late_b.start_second()
        late_a.start_second()
    with jax.named_scope("early3"):
        early.start_third()
    with jax.named_scope("halo_old_b"):
        for index in (5, 10, 11):
            arrived(index)
    with jax.named_scope("prep_old_b"):
        prepare_old(1)

    @pl.when(has_prev)
    def _():
        with jax.named_scope("conv_b"):
            conv(1)
            spread_out(1, False)

    out[pl.ds(height * rows, rows)] = pooled[height]
    with jax.named_scope("late3a"):
        late_a.start_third()

    @pl.when(jnp.logical_not(has_prev))
    def _():
        spread_out(0, True)

    with jax.named_scope("late3b"):
        late_b.start_third()
    with jax.named_scope("early4"):
        early.start_fourth()
    with jax.named_scope("late4a"):
        late_a.start_fourth()
    with jax.named_scope("late4b"):
        late_b.start_fourth()
    with jax.named_scope("last"):
        early.start_last(factor)

        @pl.when(jnp.logical_not(has_prev))
        def _():
            spread_out(1, True)


        @pl.when(has_prev)
        def _():
            spread_out(0, True)
            spread_out(1, True)

        late_a.start_last(factor)
        late_b.start_last(factor)
    with jax.named_scope("finish"):
        for stream, first, last in parts:
            wgrad[:, first:last] = stream.finish()[:, : last - first]

    with jax.named_scope("blocks_in"):
        taken(out.at[pl.ds(0, (n_rows - 1) * rows)], block_sem.at[1])
    with jax.named_scope("sent"):
        taken(out.at[pl.ds(0, (n_rows - 1) * rows)], block_sem.at[0])
        taken(stats.at[pl.ds(0, n_dev - 1)], stat_sem.at[0])
        border = full.at[own_frames, pl.ds(0, 1)]
        whole = [full.at[own_frames, pl.ds(1, rows)], border, border, border, border, cot_next]
        for index, ref in enumerate(whole):
            first = moves[SENT_BY.index(index)]
            pl.when(first[4])(functools.partial(taken, ref, halo_send.at[index]))


def deliver_kernel(block_in, grad_in, block_out, grad_out, sem):
    copies = [
        pltpu.make_async_copy(block_in, block_out, sem.at[0]),
        pltpu.make_async_copy(grad_in, grad_out, sem.at[1]),
    ]
    for copy in copies:
        copy.start()
    for copy in copies:
        copy.wait()


def local(activations, norm_gain, norm_bias, conv_weight, cotangent):
    frames, rows, width, channels = activations.shape
    depth, n_out = conv_weight.shape
    n_time, n_rows = lax.axis_size("tm"), lax.axis_size("height")
    n_dev = n_time * n_rows
    inner = 2
    outer = n_rows // (2 * inner)
    own_rows = n_out // n_rows
    dims = (n_time, n_rows, outer, inner)
    dma = pltpu.SemaphoreType.DMA
    factor = 0.5 / math.sqrt(frames * n_time * rows * n_rows * width)

    def stream(length, rows_first):
        span = -(-length // (128 * n_time)) * 128
        steps = [n_time, inner] if rows_first else [inner, n_time]
        chunk = (outer, own_rows, span)
        shapes = [
            (2, n_time, inner, *chunk),
            (n_time, inner, *chunk),
            (n_time, inner, *chunk),
            (steps[1] - 1, steps[0], *chunk),
            (steps[0], *chunk),
            (steps[0] - 1, *chunk),
            chunk,
            (outer - 1, own_rows, span),
            (own_rows, span),
            (n_time, own_rows, span),
        ]
        return [pltpu.VMEM(shape, BF16) for shape in shapes] + [dma((5,)), dma((5,))]

    band = depth // KT
    cut = 10 * channels
    out, weight_grad = pl.pallas_call(
        functools.partial(block_kernel, dims, cut, factor),
        out_shape=(
            pltpu.VMEM((rows * n_rows, own_rows, width), BF16),
            pltpu.VMEM((own_rows, depth), BF16),
        ),
        in_specs=[ANY] * 5,
        out_specs=(VMEM, VMEM),
        scratch_shapes=[
            pltpu.VMEM((2 * frames, rows + 2, width, channels), BF16),
            pltpu.VMEM((5, 2, (rows + 2) * (width // 2), KT * channels), BF16),
            pltpu.VMEM((n_out, band), F32),
            pltpu.VMEM((1, channels), F32),
            pltpu.VMEM((1, channels), F32),
            pltpu.VMEM((depth, n_out), BF16),
            pltpu.VMEM((rows, width, n_out), BF16),
            pltpu.VMEM((rows, width // 2, n_out), BF16),
            pltpu.VMEM((n_out, rows * width), BF16),
            pltpu.VMEM((n_out, rows * (width // 2)), BF16),
            pltpu.VMEM((2, channels), F32),
            pltpu.VMEM((n_dev, 2, channels), F32),
            pltpu.VMEM((n_rows, rows, own_rows, width), BF16),
            dma((5,)),
            dma((6,)),
            dma((13,)),
            dma((2,)),
            dma((2,)),
            *stream(2 * band - cut, True),
            *stream(cut, False),
            *stream(band, True),
        ],
        compiler_params=pltpu.CompilerParams(collective_id=0, has_side_effects=True, vmem_limit_bytes=60 << 20),
        name="block",
    )(
        activations,
        norm_gain.reshape(1, channels),
        norm_bias.reshape(1, channels),
        conv_weight,
        cotangent.reshape(rows, width, n_out),
    )
    out, weight_grad = pl.pallas_call(
        deliver_kernel,
        out_shape=(
            jax.ShapeDtypeStruct(out.shape, BF16),
            jax.ShapeDtypeStruct(weight_grad.shape, BF16),
        ),
        in_specs=[ANY] * 2,
        out_specs=(ANY, ANY),
        scratch_shapes=[dma((2,))],
        compiler_params=pltpu.CompilerParams(vmem_limit_bytes=4 << 20),
        name="deliver",
    )(out, weight_grad)
    return (out.reshape((1,) + out.shape), weight_grad)


def solution(mesh):
    in_specs = (P("tm", "height", None, None), P(), P(), P(), P("tm", "height", None, None))
    out_specs = (P("tm", None, "height", None), P("height", None))
    return jax.shard_map(local, mesh=mesh, in_specs=in_specs, out_specs=out_specs, check_vma=False)
```
